32 devices in a mesh: track: 16 (over z, x, core), head: 2 (over y).
Axes of the slice: x: 2, y: 2, z: 4, core: 2. Of those that a mesh axis runs over, the one named last changes fastest.
Arguments:
- residual_in: bfloat16 [16, 256, 2048], P('track', None, 'head')
- queries: bfloat16 [16, 256, 2048], P('track', None, 'head')
- key_vectors: bfloat16 [16, 256, 2048], P('track', None, 'head')
- values: bfloat16 [16, 256, 2048], P('track', None, 'head'), may hold values from -24 to 24
- bar_index: int32 [16, 256], replicated, may hold values from 0 to 31, as said below
- pair_offset: int32 [16, 16, 4], replicated, may hold values from 0 to 14, all different within a row; in each aligned block of 16 rows (0 to 15, 16 to 31, ..., all dimensions but the last counted through in order) at most 8 rows name the same one
- out_proj: bfloat16 [2048, 2048], P('head'), may hold values from -0.125 to 0.125
- norm_gain: bfloat16 [2048], P('head'), may hold values from 0.099609375 to 1.8984375
- router: bfloat16 [2048, 16], P('head'), may hold values from -0.125 to 0.125
- expert_route: int32 [16, 256, 2], P('track'), may hold values from 0 to 15, all different within a row; in each aligned block of 256 rows (0 to 255, 256 to 511, ..., all dimensions but the last counted through in order) at most 64 rows name the same one
- w_gate: bfloat16 [16, 2048, 1408], P('track', None, 'head'), may hold values from -0.125 to 0.125
- w_up: bfloat16 [16, 2048, 1408], P('track', None, 'head'), may hold values from -0.125 to 0.125
- w_down: bfloat16 [16, 1408, 2048], P('track', 'head'), may hold values from -0.15625 to 0.15625
Outputs:
- layer_out: bfloat16 [16, 256, 2048], P('track', None, 'head')
The draws below stay inside these ranges and needn't reach their ends.
Inputs may be any that keep to these rules, and one draw needn't show every extreme that they name: bar_index[t, 0] = 0, and along a track each event's bar equals the one before or exceeds it by 1; the largest value is reached in every draw. `pair_offset`: the 4 entries of one query block differ; among the 16 query blocks of one track no value appears more than 8 times, and in every draw some track has a value that appears exactly 8 times. `expert_route`: the 2 entries of an event differ; among the 256 events of one track no expert appears more than 64 times, and in every draw some track has an expert that appears exactly 64 times.
All inputs are finite; a program needn't handle non-finite values.
Results may differ from the reference program's by a relative error of at most 0.0054.
Values may be sent and summed in bfloat16 or wider, within the bound.
No kernel may reach another device: no remote copies, remote signals or barrier semaphores. Data moves between devices by JAX's collectives and lax.ppermute only.
A program may use at most 256 MiB of HBM per device.

```python
import math
import jax
import jax.numpy as jnp
import numpy as np
from jax import lax

D = 2048
HEADS = 16
FF = 1408
TOK_DEV = 256
QB = 16
PAIRS = 4
BAND = 2
TOP = 2
HEAD_DIM = 128
TRACKS = 16
EXPERTS = 16
NQB = 16
PCAP = 8
CAP = 64
FF_PART = 704


def shared_query_keys(key):
    base = jax.random.fold_in(key, 1701)
    key_part = jax.random.normal(jax.random.fold_in(base, 1), (TRACKS, TOK_DEV, D), jnp.float32)
    query_part = jax.random.normal(jax.random.fold_in(base, 2), (TRACKS, TOK_DEV, D), jnp.float32)
    return (query_part, key_part)


def draw_queries(key, part):
    return shared_query_keys(key)[0].astype(jnp.bfloat16)


def draw_key_vectors(key, part):
    return shared_query_keys(key)[1].astype(jnp.bfloat16)


def draw_residual_in(key, part):
    base = jax.random.fold_in(key, 2203)
    shape = (TRACKS, TOK_DEV, D)
    noise = jax.random.normal(jax.random.fold_in(base, 1), shape, jnp.float32)
    row_low, row_high = (-1.2, 1.1)
    ramp = jnp.log(3.0) * jnp.arange(D, dtype=jnp.float32) / (D - 1)
    column = 0.6 * jnp.exp(ramp + jax.random.uniform(jax.random.fold_in(base, 2), (D,), jnp.float32, -0.35, 0.35))
    row_scale = jnp.exp(jax.random.uniform(jax.random.fold_in(base, 3), (TRACKS, TOK_DEV, 1), jnp.float32, row_low, row_high))
    return (noise * column * row_scale).astype(jnp.bfloat16)


def draw_bar_index(key, part):
    base = jax.random.fold_in(key, 3307)
    spacing = jax.random.randint(jax.random.fold_in(base, 1), (TRACKS, 1), 8, 25)
    ticks = jax.random.randint(jax.random.fold_in(base, 2), (TRACKS, TOK_DEV), 0, 1 << 20)
    steps_up = jnp.where(jnp.arange(TOK_DEV)[None, :] == 0, 0, (ticks % spacing == 0).astype(jnp.int32))
    ragged = jnp.cumsum(steps_up, axis=1).astype(jnp.int32)
    regular = (jnp.arange(TOK_DEV, dtype=jnp.int32) // 8)[None, :]
    capped = jnp.minimum(ragged, regular)
    full_track = jax.random.randint(jax.random.fold_in(base, 3), (), 0, TRACKS)
    is_full = (jnp.arange(TRACKS, dtype=jnp.int32) == full_track)[:, None]
    return jnp.where(is_full, regular, capped).astype(jnp.int32)


def levels(rng, shape, cuts, smallest, high):
    gain, own = 1.0, jax.random.fold_in(rng, 6)
    for dim, parts in cuts:
        draws = jnp.exp(jax.random.uniform(jax.random.fold_in(own, dim), (parts,), jnp.float32, smallest / len(cuts), high / len(cuts)))
        gain = gain * jnp.repeat(draws, shape[dim] // parts).reshape([-1 if axis == dim else 1 for axis in range(len(shape))])
    return gain


def routed_block(key, own, number, rows, count, top, most, skew):
    ranking = jax.random.permutation(key, count)
    packed, ordinary = load_shares(count, rows * top, most, skew, True), load_shares(count, rows * top, most, skew, False)
    places = jnp.arange(count)

    def named(lengths, rotation):
        used = int((lengths > 0).sum())
        fixed = max(1, used // 4)
        moved = fixed + (places - fixed + rotation * (used - fixed)) % max(1, count - fixed)
        return jnp.zeros((count,), jnp.int32).at[ranking[jnp.where(places < fixed, places, moved)]].set(jnp.asarray(lengths, jnp.int32))

    lengths = jnp.where(number % 4 == 0, named(packed, number // 4), named(ordinary, number - number // 4 - 1))
    mixed = jax.random.permutation(jax.random.fold_in(own, 3), count)
    donor, receiver = mixed[0:count // 2 * 2:2], mixed[1:count // 2 * 2:2]
    room = jnp.minimum(lengths[donor] - 1, most - lengths[receiver]) // 2
    room = jnp.where((donor == ranking[0]) | (receiver == ranking[0]) | (lengths[receiver] == 0), 0, jnp.maximum(room, 0))
    moved = jax.random.randint(jax.random.fold_in(own, 4), (count // 2,), 0, 1 << 20) % (room + 1)
    lengths = lengths.at[donor].add(-moved).at[receiver].add(moved)
    members = jnp.searchsorted(jnp.cumsum(lengths), jnp.arange(rows * top), side="right").astype(jnp.int32)
    grid = members.reshape(top, rows).T
    grid = grid[jax.random.permutation(jax.random.fold_in(own, 1), rows)]
    rotation = jax.random.randint(jax.random.fold_in(own, 2), (rows, 1), 0, top)
    return jnp.take_along_axis(grid, (jnp.arange(top)[None, :] + rotation) % top, axis=1)


def load_shares(amount, total, limit, lean, full):
    portions = [(1 << 20) // math.isqrt(grade ** lean) + 1 for grade in range(1, amount + 1)]
    largest = limit if full else min(limit, max(-(-total // amount), total * portions[0] // sum(portions)))
    least = 1 if total - largest >= amount - 1 else 0
    counts, rest = [largest] + [least] * (amount - 1), total - largest - least * (amount - 1)
    while rest > 0:
        free = [i for i in range(1, amount) if counts[i] < largest] or [i for i in range(1, amount) if counts[i] < limit]
        mass, left = sum([portions[i] for i in free]), rest
        for i in free:
            addition = min(limit - counts[i], max(1, left * portions[i] // mass), rest)
            counts[i] = counts[i] + addition
            rest = rest - addition
    return np.array(counts)


def normal_values(key, shape, scale, reach, pieces=(), kind=jnp.bfloat16):
    entries = scale * jax.random.normal(key, shape, jnp.float32)
    if pieces:
        entries = entries * levels(key, shape, pieces, -0.22, 0.18)
    return jnp.clip(entries, -reach, reach).astype(kind)


def setup_inputs(seed: int = 0) -> dict:
    key_list = jax.random.split(jax.random.key(seed), 14)
    residual_in = draw_residual_in(jax.random.fold_in(key_list[13], 71), 0)
    queries = draw_queries(jax.random.fold_in(key_list[13], 71), 0)
    key_vectors = draw_key_vectors(jax.random.fold_in(key_list[13], 71), 0)
    values = normal_values(key_list[3], (TRACKS, TOK_DEV, D), 4.0, 24.0, ((0, 16), (2, 2)))
    bar_index = draw_bar_index(jax.random.fold_in(key_list[13], 71), 0)
    pair_offset_keys = jax.random.split(jax.random.fold_in(key_list[5], 1), TRACKS * NQB // NQB)
    pair_offset_turns = jax.random.permutation(jax.random.fold_in(key_list[5], 3), TRACKS * NQB // NQB)
    pair_offset = jax.vmap(lambda own, number: routed_block(jax.random.fold_in(key_list[5], 2), own, number, NQB, TRACKS - 1, PAIRS, PCAP, 2))(pair_offset_keys, pair_offset_turns).reshape((TRACKS, NQB, PAIRS))
    out_proj = normal_values(key_list[6], (D, D), D ** -0.5, 0.125, ((0, 2),))
    norm_gain = jnp.clip(1.0 + 0.18 * jax.random.normal(key_list[7], (D,), jnp.float32), 0.099609375, 1.8984375).astype(jnp.bfloat16)
    router = normal_values(key_list[8], (D, EXPERTS), D ** -0.5, 0.125, ((0, 2),))
    expert_route_keys = jax.random.split(jax.random.fold_in(key_list[9], 1), TRACKS * TOK_DEV // TOK_DEV)
    expert_route_turns = jax.random.permutation(jax.random.fold_in(key_list[9], 3), TRACKS * TOK_DEV // TOK_DEV)
    expert_route = jax.vmap(lambda own, number: routed_block(jax.random.fold_in(key_list[9], 2), own, number, TOK_DEV, EXPERTS, TOP, CAP, 2))(expert_route_keys, expert_route_turns).reshape((TRACKS, TOK_DEV, TOP))
    w_gate = normal_values(key_list[10], (EXPERTS, D, FF), D ** -0.5, 0.125, ((0, 16), (2, 2)))
    w_up = normal_values(key_list[11], (EXPERTS, D, FF), D ** -0.5, 0.125, ((0, 16), (2, 2)))
    w_down = normal_values(key_list[12], (EXPERTS, FF, D), FF ** -0.5, 0.15625, ((0, 16), (1, 2)))
    return {"residual_in": residual_in, "queries": queries, "key_vectors": key_vectors, "values": values, "bar_index": bar_index, "pair_offset": pair_offset, "out_proj": out_proj, "norm_gain": norm_gain, "router": router, "expert_route": expert_route, "w_gate": w_gate, "w_up": w_up, "w_down": w_down}


MASKED_SCORE = -1e+30
NORM_EPSILON = 1e-06

def masked_softmax_parts(scores, allowed):
    ceiling = lax.optimization_barrier(jnp.max(jnp.where(allowed, scores, MASKED_SCORE), axis=-1))
    weights = jnp.where(allowed, jnp.exp(scores - ceiling[..., None]), 0.0)
    return (ceiling, lax.optimization_barrier(jnp.sum(weights, axis=-1)), weights.astype(jnp.bfloat16))

def merge_sets(self_peak, self_mass, self_value, pair_peak, pair_mass, pair_value):
    ceiling = jnp.maximum(self_peak, lax.optimization_barrier(jnp.max(pair_peak, axis=1)))
    self_scale = jnp.exp(self_peak - ceiling)
    pair_scale = jnp.exp(pair_peak - ceiling[:, None])
    numerator = self_scale[..., None] * self_value + lax.optimization_barrier(jnp.sum(pair_scale[..., None] * pair_value, axis=1))
    denominator = self_scale * self_mass + lax.optimization_barrier(jnp.sum(pair_scale * pair_mass, axis=1))
    return numerator / denominator[..., None]

def reference(residual_in, queries, key_vectors, values, bar_index, pair_offset, out_proj, norm_gain, router, expert_route, w_gate, w_up, w_down):
    score_scale = 1.0 / HEAD_DIM ** 0.5
    position = jnp.arange(TOK_DEV, dtype=jnp.int32)

    def track_attention(track_id):
        own_query = queries[track_id].reshape(TOK_DEV, HEADS, HEAD_DIM).astype(jnp.float32)
        own_keys = key_vectors[track_id].reshape(TOK_DEV, HEADS, HEAD_DIM).astype(jnp.float32)
        own_values = values[track_id].reshape(TOK_DEV, HEADS, HEAD_DIM).astype(jnp.float32)
        own_bars = bar_index[track_id]
        self_allowed = (own_bars[None, :] <= own_bars[:, None]) & (own_bars[None, :] >= own_bars[:, None] - BAND) & (position[None, :] <= position[:, None])
        scores = jnp.einsum('qhd,khd->hqk', own_query, own_keys) * score_scale
        self_peak, self_mass, self_weights = masked_softmax_parts(scores, self_allowed[None])
        self_value = jnp.einsum('hqk,khd->qhd', self_weights.astype(jnp.float32), own_values)
        self_peak = jnp.moveaxis(self_peak, 0, -1).reshape(NQB, QB, HEADS)
        self_mass = jnp.moveaxis(self_mass, 0, -1).reshape(NQB, QB, HEADS)
        self_value = self_value.reshape(NQB, QB, HEADS, HEAD_DIM)
        partners = ((track_id + 1 + pair_offset[track_id]) % TRACKS).astype(jnp.int32)
        far_keys = key_vectors[partners].reshape(NQB, PAIRS, TOK_DEV, HEADS, HEAD_DIM).astype(jnp.float32)
        far_values = values[partners].reshape(NQB, PAIRS, TOK_DEV, HEADS, HEAD_DIM).astype(jnp.float32)
        far_bars = bar_index[partners]
        query_bars = own_bars.reshape(NQB, QB)
        block_query = own_query.reshape(NQB, QB, HEADS, HEAD_DIM)
        far_scores = jnp.einsum('bqhd,bjkhd->bjhqk', block_query, far_keys) * score_scale
        far_allowed = (far_bars[:, :, None, :] <= query_bars[:, None, :, None]) & (far_bars[:, :, None, :] >= query_bars[:, None, :, None] - BAND)
        pair_peak, pair_mass, pair_weights = masked_softmax_parts(far_scores, far_allowed[:, :, None])
        pair_value = jnp.einsum('bjhqk,bjkhd->bjqhd', pair_weights.astype(jnp.float32), far_values)
        pair_peak = jnp.moveaxis(pair_peak, 2, -1)
        pair_mass = jnp.moveaxis(pair_mass, 2, -1)
        merged = merge_sets(self_peak, self_mass, self_value, pair_peak, pair_mass, pair_value)
        return merged.reshape(TOK_DEV, D).astype(jnp.bfloat16)
    attended = lax.map(track_attention, jnp.arange(TRACKS, dtype=jnp.int32))
    projected = jnp.dot(attended.reshape(TRACKS * TOK_DEV, D), out_proj, preferred_element_type=jnp.float32).reshape(TRACKS, TOK_DEV, D)
    hidden = (residual_in.astype(jnp.float32) + projected).astype(jnp.bfloat16)
    hidden_wide = lax.optimization_barrier(hidden).astype(jnp.float32)
    mean_square = lax.optimization_barrier(jnp.sum(hidden_wide * hidden_wide, axis=-1, keepdims=True)) / D
    normed = (hidden_wide * lax.rsqrt(mean_square + NORM_EPSILON) * norm_gain.astype(jnp.float32)).astype(jnp.bfloat16)
    logits = jnp.dot(normed.reshape(TRACKS * TOK_DEV, D), router, preferred_element_type=jnp.float32).reshape(TRACKS, TOK_DEV, EXPERTS)
    matches = expert_route[..., None] == jnp.arange(EXPERTS, dtype=jnp.int32)
    chosen = lax.optimization_barrier(jnp.sum(jnp.where(matches, logits[:, :, None, :], 0.0), axis=-1))
    sigmoid_vals = jax.nn.sigmoid(chosen)
    gate_share = sigmoid_vals / lax.optimization_barrier(jnp.sum(sigmoid_vals, axis=-1, keepdims=True))
    flat_route = expert_route.reshape(TRACKS, TOK_DEV * TOP)
    route_hits = (flat_route[..., None] == jnp.arange(EXPERTS, dtype=jnp.int32)).astype(jnp.int32)
    slot_rank = lax.optimization_barrier(jnp.sum((jnp.cumsum(route_hits, axis=1) - route_hits) * route_hits, axis=-1)).astype(jnp.int32)
    token_of = jnp.arange(TOK_DEV * TOP, dtype=jnp.int32) // TOP
    track_ids = jnp.arange(TRACKS, dtype=jnp.int32)[:, None]
    buffers = jnp.zeros((EXPERTS, TRACKS, CAP, D), jnp.bfloat16).at[flat_route, track_ids, slot_rank].set(normed[:, token_of])

    def run_expert(expert_id):
        expert_rows = buffers[expert_id].reshape(TRACKS * CAP, D)
        gate_pre = jnp.dot(expert_rows, w_gate[expert_id], preferred_element_type=jnp.float32)
        up_pre = jnp.dot(expert_rows, w_up[expert_id], preferred_element_type=jnp.float32)
        activated = (jax.nn.silu(gate_pre) * up_pre).astype(jnp.bfloat16)
        groups = FF // FF_PART
        down_terms = jnp.einsum('rqf,qfd->qrd', activated.reshape(TRACKS * CAP, groups, FF_PART).astype(jnp.float32), w_down[expert_id].reshape(groups, FF_PART, D).astype(jnp.float32))
        down_terms = lax.optimization_barrier(down_terms.astype(jnp.bfloat16)).astype(jnp.float32)
        return lax.optimization_barrier(jnp.sum(down_terms, axis=0)).astype(jnp.bfloat16).reshape(TRACKS, CAP, D)
    expert_out = lax.map(run_expert, jnp.arange(EXPERTS, dtype=jnp.int32))
    picked = expert_out[flat_route, track_ids, slot_rank].reshape(TRACKS, TOK_DEV, TOP, D).astype(jnp.float32)
    return (hidden_wide + lax.optimization_barrier(jnp.sum(gate_share[..., None] * picked, axis=2))).astype(jnp.bfloat16)
```

```python
import functools
import math

import jax
import jax.numpy as jnp
from jax import lax
from jax.experimental import pallas as pl
from jax.experimental.pallas import tpu as pltpu
from jax.sharding import PartitionSpec as P

D = 2048
QB = 16
PAIRS = 4
BAND = 2
TOP = 2
HEAD_DIM = 128
HEAD_CHUNKS = 2
SLOT_CHUNKS = 4
LANES = 128

MASKED_SCORE = -1e30
NO_CAP = 3e38
NORM_EPSILON = 1e-06
F32 = jnp.float32
BF16 = jnp.bfloat16


def dot(a, b):
    return jnp.dot(a, b, preferred_element_type=F32)


def dot_nt(a, b):
    return lax.dot_general(a, b, (((1,), (1,)), ((), ())), preferred_element_type=F32)


def chip_ring(rows, columns):
    order = []
    for row in range(rows):
        inner = list(range(1, columns))
        order += [(row, x) for x in (inner if row % 2 == 0 else inner[::-1])]
    order += [(row, 0) for row in range(rows - 1, -1, -1)]
    return [z * columns + x for z, x in order]


def shifted(x, axis, size, shift):
    return lax.ppermute(x, axis, [(i, (i + shift) % size) for i in range(size)])


def swap_cores(x, tracks):
    return lax.ppermute(x, "track", [(i, i ^ 1) for i in range(tracks)])


def attention_kernel(blocks, heads, *refs):
    q_ref, qbar_ref, kbar_ref = refs[:3]
    kv_refs = refs[3 : 3 + blocks]
    own_ref, other_ref, cap_ref = refs[3 + blocks :]
    head = pl.program_id(0)
    events = q_ref.shape[1]
    exponent_scale = math.log2(math.e) / math.sqrt(HEAD_DIM)
    tile = 128

    @pl.when(head == 0)
    def _():
        row = lax.broadcasted_iota(jnp.int32, (events, events), 0)
        column = lax.broadcasted_iota(jnp.int32, (events, events), 1)
        for side in range(2):
            for b in range(blocks):
                back = qbar_ref[side, :, b : b + 1] - kbar_ref[b : b + 1, :]
                allowed = (back >= 0) & (back <= BAND)
                if side == 0 and b == 0:
                    allowed = allowed & (column <= row)
                cap_ref[side, :, b * events : (b + 1) * events] = jnp.where(
                    allowed, NO_CAP, MASKED_SCORE
                )

    lane = lax.broadcasted_iota(jnp.int32, (tile, LANES), 1)
    for side, out_ref in enumerate((own_ref, other_ref)):
        for start in range(0, events, tile):
            rows = pl.ds(start, tile)
            query = q_ref[side, rows, :]
            scores = [
                jnp.minimum(
                    dot_nt(query, kv_refs[b][0]), cap_ref[side, rows, b * events : (b + 1) * events]
                )
                for b in range(blocks)
            ]
            peak = functools.reduce(jnp.maximum, scores).max(axis=1, keepdims=True)
            mass = jnp.zeros((tile, events), F32)
            value = jnp.zeros((tile, HEAD_DIM), F32)
            for b in range(blocks):
                weights = jnp.exp2((scores[b] - peak) * exponent_scale)
                mass = mass + weights
                value = value + dot(weights.astype(BF16), kv_refs[b][1])
            mass = mass.sum(axis=1, keepdims=True)
            out_ref[rows, pl.ds(pl.multiple_of(head * HEAD_DIM, HEAD_DIM), HEAD_DIM)] = value
            stat = jnp.where(lane == head, peak, jnp.where(lane == heads + head, mass, 0.0))

            @pl.when(head == 0)
            def _():
                out_ref[rows, heads * HEAD_DIM :] = stat

            @pl.when(head != 0)
            def _():
                out_ref[rows, heads * HEAD_DIM :] += stat


def attention(q, qbar, kbar, kvs):
    blocks, events, width = len(kvs), q.shape[1], q.shape[2]
    heads = width // HEAD_DIM
    shape = jax.ShapeDtypeStruct((events, width + LANES), F32)
    flops = 4 * 2 * events * blocks * events * width
    return pl.pallas_call(
        functools.partial(attention_kernel, blocks, heads),
        grid=(heads,),
        in_specs=[
            pl.BlockSpec((2, events, HEAD_DIM), lambda h: (0, 0, h)),
            pl.BlockSpec(qbar.shape, lambda h: (0, 0, 0)),
            pl.BlockSpec(kbar.shape, lambda h: (0, 0)),
        ]
        + [pl.BlockSpec((2, events, HEAD_DIM), lambda h: (0, 0, h))] * blocks,
        out_specs=[pl.BlockSpec(shape.shape, lambda h: (0, 0))] * 2,
        out_shape=[shape, shape],
        scratch_shapes=[pltpu.VMEM((2, events, blocks * events), F32)],
        cost_estimate=pl.CostEstimate(
            flops=flops, bytes_accessed=blocks * events * width * 4, transcendentals=flops // 512
        ),
        name="attention",
    )(q, qbar, kbar, *kvs)


def merge_kernel(heads, a_ref, b_ref, out_ref):
    scale = 1.0 / math.sqrt(HEAD_DIM)
    for head in range(heads):
        at = heads * HEAD_DIM + head
        peak_a, mass_a = a_ref[:, at : at + 1], a_ref[:, at + heads : at + heads + 1]
        peak_b, mass_b = b_ref[:, at : at + 1], b_ref[:, at + heads : at + heads + 1]
        peak = jnp.maximum(peak_a, peak_b)
        scale_a = jnp.exp((peak_a - peak) * scale)
        scale_b = jnp.exp((peak_b - peak) * scale)
        part = slice(head * HEAD_DIM, (head + 1) * HEAD_DIM)
        total = scale_a * a_ref[:, part] + scale_b * b_ref[:, part]
        out_ref[:, part] = (total / (scale_a * mass_a + scale_b * mass_b)).astype(BF16)


def merge(a, b):
    events, width = a.shape[0], a.shape[1] - LANES
    return pl.pallas_call(
        functools.partial(merge_kernel, width // HEAD_DIM),
        out_shape=jax.ShapeDtypeStruct((events, width), BF16),
        cost_estimate=pl.CostEstimate(
            flops=8 * events * width, bytes_accessed=10 * events * width, transcendentals=0
        ),
        name="merge",
    )(a, b)


def project_kernel(sources, chunks, experts, *refs):
    attended = refs[: sources * chunks]
    weights = refs[sources * chunks : sources * chunks + sources]
    residual_ref, gain_ref, router_ref, hidden_ref, stat_ref = refs[sources * chunks + sources :]
    step = pl.program_id(0)
    total = residual_ref[...].astype(F32)
    for source in range(sources):
        for chunk in range(chunks):
            part = attended[source * chunks + chunk][...]
            width = part.shape[1]
            total = total + dot(part, weights[source][chunk * width : (chunk + 1) * width, :])
    hidden = total.astype(BF16)
    hidden_ref[...] = hidden
    wide = hidden.astype(F32)
    scaled = (wide * gain_ref[...].astype(F32)).astype(BF16)
    lane = lax.broadcasted_iota(jnp.int32, stat_ref.shape, 1)
    square = jnp.sum(wide * wide, axis=1, keepdims=True)
    stat = dot(scaled, router_ref[...]) + jnp.where(lane == experts, square, 0.0)

    @pl.when(step == 0)
    def _():
        stat_ref[...] = stat

    @pl.when(step != 0)
    def _():
        stat_ref[...] += stat


def project(attended, weights, residual, gain, router, experts):
    events, width = residual.shape
    sources, chunks = len(attended), len(attended[0])
    tile = 256
    flat = [part for source in attended for part in source]
    return pl.pallas_call(
        functools.partial(project_kernel, sources, chunks, experts),
        grid=(width // tile,),
        in_specs=[pl.BlockSpec(part.shape, lambda j: (0, 0)) for part in flat]
        + [pl.BlockSpec((w.shape[0], tile), lambda j: (0, j)) for w in weights]
        + [
            pl.BlockSpec((events, tile), lambda j: (0, j)),
            pl.BlockSpec((1, tile), lambda j: (0, j)),
            pl.BlockSpec((tile, LANES), lambda j: (j, 0)),
        ],
        out_specs=[
            pl.BlockSpec((events, tile), lambda j: (0, j)),
            pl.BlockSpec((events, LANES), lambda j: (0, 0)),
        ],
        out_shape=[
            jax.ShapeDtypeStruct((events, width), BF16),
            jax.ShapeDtypeStruct((events, LANES), F32),
        ],
        cost_estimate=pl.CostEstimate(
            flops=2 * events * D * width, bytes_accessed=2 * D * width, transcendentals=0
        ),
        name="project",
    )(*flat, *weights, residual, gain, router)


def pack_kernel(sources, chunks, experts, *refs):
    hidden_ref = refs[0]
    stats = refs[1 : 1 + sources]
    gain_ref, route_ref, code_ref = refs[1 + sources : 4 + sources]
    outs = refs[4 + sources : 4 + sources + chunks]
    gate_ref = refs[4 + sources + chunks]
    total = functools.reduce(jnp.add, [s[...] for s in stats])
    lane = lax.broadcasted_iota(jnp.int32, total.shape, 1)
    square = jnp.sum(jnp.where(lane == experts, total, 0.0), axis=1, keepdims=True)
    inverse = lax.rsqrt(square / D + NORM_EPSILON)
    normed = (hidden_ref[...].astype(F32) * inverse * gain_ref[...].astype(F32)).astype(BF16)
    rows, events = outs[0].shape[0], normed.shape[0]
    tile = min(rows, 256)
    row = lax.broadcasted_iota(jnp.int32, (tile, events), 0)
    for chunk in range(chunks):
        for start in range(0, rows, tile):
            at = row + (chunk * rows + start)
            hit = (code_ref[0:1, :] == at) | (code_ref[1:2, :] == at)
            pick = jnp.where(hit, 1.0, 0.0).astype(BF16)
            outs[chunk][start : start + tile, :] = dot(pick, normed).astype(BF16)
    logits = total * inverse
    parts = []
    for k in range(TOP):
        chosen = jnp.sum(
            jnp.where(lane == route_ref[:, k : k + 1], logits, 0.0), axis=1, keepdims=True
        )
        parts.append(1.0 / (1.0 + jnp.exp(-chosen)))
    whole = parts[0] + parts[1]
    gate_ref[...] = jnp.where(
        lane == 0, parts[0] / whole, jnp.where(lane == 1, parts[1] / whole, 0.0)
    )


def pack(hidden, stats, gain, route, code_rows, chunks, rows, experts):
    events, width = hidden.shape
    out = jax.ShapeDtypeStruct((rows, width), BF16)
    return pl.pallas_call(
        functools.partial(pack_kernel, len(stats), chunks, experts),
        out_shape=[out] * chunks + [jax.ShapeDtypeStruct((events, LANES), F32)],
        cost_estimate=pl.CostEstimate(
            flops=2 * events * chunks * rows * width,
            bytes_accessed=2 * chunks * rows * width,
            transcendentals=0,
        ),
        name="pack",
    )(hidden, *stats, gain, route, code_rows)


def expert_in_kernel(sources, per_source, kmap_ref, *refs):
    rows = refs[:sources]
    gate_ref, up_ref, out_ref, gate_sum, up_sum = refs[sources:]
    step = pl.program_id(0)

    @pl.when(step == 0)
    def _():
        gate_sum[...] = jnp.zeros_like(gate_sum)
        up_sum[...] = jnp.zeros_like(up_sum)

    for source in range(sources):

        @pl.when(step // per_source == source)
        def _():
            x = rows[source][...]
            gate_sum[...] += dot(x, gate_ref[0])
            up_sum[...] += dot(x, up_ref[0])

    @pl.when(step == pl.num_programs(0) - 1)
    def _():
        gate = gate_sum[...]
        out_ref[...] = (gate / (1.0 + jnp.exp(-gate)) * up_sum[...]).astype(BF16)


def expert_in(rows, w_gate, w_up, my_head):
    sources = len(rows)
    count, width = rows[0].shape
    units = w_gate.shape[2]
    tile = 512
    per_source = width // tile
    steps = sources * per_source
    number = jnp.arange(steps, dtype=jnp.int32)
    kmap = (my_head - number // per_source + sources) % sources * per_source + number % per_source

    def row_map(source):
        return lambda k, m: (0, jnp.clip(k - source * per_source, 0, per_source - 1))

    weight = pl.BlockSpec((1, tile, units), lambda k, m: (0, m[k], 0))
    return pl.pallas_call(
        functools.partial(expert_in_kernel, sources, per_source),
        grid_spec=pltpu.PrefetchScalarGridSpec(
            num_scalar_prefetch=1,
            grid=(steps,),
            in_specs=[pl.BlockSpec((count, tile), row_map(s)) for s in range(sources)]
            + [weight, weight],
            out_specs=pl.BlockSpec((count, units), lambda k, m: (0, 0)),
            scratch_shapes=[pltpu.VMEM((count, units), F32)] * 2,
        ),
        out_shape=jax.ShapeDtypeStruct((count, units), BF16),
        cost_estimate=pl.CostEstimate(
            flops=4 * count * D * units, bytes_accessed=4 * D * units, transcendentals=count * units
        ),
        name="expert_in",
    )(kmap, *rows, w_gate, w_up)


def expert_out_kernel(sources, *refs):
    out_ref = refs[2 * sources]
    total = dot(refs[0][...], refs[sources][...])
    for s in range(1, sources):
        total = total + dot(refs[s][...], refs[sources + s][...])
    out_ref[...] = total.astype(BF16)


def expert_out(acts, weights):
    sources = len(acts)
    count, units = acts[0].shape
    width = weights[0].shape[1]
    tile = 256
    return pl.pallas_call(
        functools.partial(expert_out_kernel, sources),
        grid=(width // tile,),
        in_specs=[pl.BlockSpec((count, units), lambda j: (0, 0))] * sources
        + [pl.BlockSpec((units, tile), lambda j: (0, j))] * sources,
        out_specs=pl.BlockSpec((count, tile), lambda j: (0, j)),
        out_shape=jax.ShapeDtypeStruct((count, width), BF16),
        cost_estimate=pl.CostEstimate(
            flops=2 * sources * count * units * width,
            bytes_accessed=2 * sources * units * width,
            transcendentals=0,
        ),
        name="expert_out",
    )(*acts, *weights)


def combine_kernel(chunks, *refs):
    hidden_ref, gate_ref, code_ref = refs[:3]
    returned = refs[3 : 3 + chunks]
    out_ref = refs[3 + chunks]
    total = hidden_ref[...].astype(F32)
    events, rows = total.shape[0], returned[0].shape[0]
    column = lax.broadcasted_iota(jnp.int32, (events, rows), 1)
    picked = [None] * TOP
    for chunk in range(chunks):
        back = returned[chunk][...]
        for k in range(TOP):
            hit = column + chunk * rows == code_ref[:, k : k + 1]
            part = dot(jnp.where(hit, 1.0, 0.0).astype(BF16), back)
            picked[k] = part if chunk == 0 else picked[k] + part
    share = picked[0] * gate_ref[:, 0:1]
    for k in range(1, TOP):
        share = share + picked[k] * gate_ref[:, k : k + 1]
    out_ref[...] = (total + share).astype(BF16)


def combine(hidden, gates, code_columns, returned):
    events, width = hidden.shape
    chunks, rows = len(returned), returned[0].shape[0]
    return pl.pallas_call(
        functools.partial(combine_kernel, chunks),
        out_shape=jax.ShapeDtypeStruct((events, width), BF16),
        cost_estimate=pl.CostEstimate(
            flops=4 * events * chunks * rows * width,
            bytes_accessed=2 * chunks * rows * width,
            transcendentals=0,
        ),
        name="combine",
    )(hidden, gates, code_columns, *returned)


def local(
    order,
    residual_in,
    queries,
    key_vectors,
    values,
    bar_index,
    pair_offset,
    out_proj,
    norm_gain,
    router,
    expert_route,
    w_gate,
    w_up,
    w_down,
):
    tracks = lax.axis_size("track")
    head_parts = lax.axis_size("head")
    my_track = lax.axis_index("track")
    my_head = lax.axis_index("head")
    events, width = queries.shape[1], queries.shape[2]
    chips = len(order)
    shifts = range(1, head_parts)

    def columns_of(weight, owner):
        return lax.dynamic_slice_in_dim(weight, owner * width, width, 1)

    out_weights = [columns_of(out_proj, my_head)]
    down_weights = [columns_of(w_down[0], my_head)]
    for s in shifts:
        owner = (my_head + s) % head_parts
        out_weights.append(shifted(columns_of(out_proj, owner), "head", head_parts, s))
        down_weights.append(shifted(columns_of(w_down[0], owner), "head", head_parts, s))

    forward = [
        (2 * order[i] + c, 2 * order[(i + 1) % chips] + c) for i in range(chips) for c in range(2)
    ]
    backward = [(b, a) for a, b in forward]
    chunk_width = width // HEAD_CHUNKS
    both_queries = jnp.concatenate([queries, swap_cores(queries, tracks)], axis=0)
    rings = []
    for chunk in range(HEAD_CHUNKS):
        part = slice(chunk * chunk_width, (chunk + 1) * chunk_width)
        block = jnp.concatenate([key_vectors[:, :, part], values[:, :, part]], axis=0)
        got, ahead, back = [block], block, block
        for _ in range(chips // 2 - 1):
            ahead = lax.ppermute(ahead, "track", forward)
            back = lax.ppermute(back, "track", backward)
            got += [ahead, back]
        if chunk % 2 == 0:
            got.append(lax.ppermute(ahead, "track", forward))
        else:
            got.append(lax.ppermute(back, "track", backward))
        rings.append(got)
    hops = [0]
    for s in range(1, chips // 2):
        hops += [-s, s]
    hops.append(chips // 2)

    place = [0] * chips
    for i, chip in enumerate(order):
        place[chip] = i
    my_place = jnp.array(place, jnp.int32)[my_track // 2]
    block_chip = jnp.array(order, jnp.int32)[(my_place + jnp.array(hops, jnp.int32)) % chips]
    block_track = block_chip * 2 + my_track % 2
    key_bars = bar_index[block_track]
    query_track = jnp.stack([my_track, my_track ^ 1])
    query_bars = bar_index[query_track]
    partner = (query_track[:, None, None] + 1 + pair_offset[query_track]) % tracks
    listed = jnp.any(partner[:, :, :, None] == block_track, axis=2)
    listed = listed | (query_track[:, None, None] == block_track)
    listed = jnp.repeat(listed, QB, axis=1)
    query_bars = jnp.where(listed, query_bars[:, :, None], -1000)

    attended = [[] for _ in range(head_parts)]
    for chunk in range(HEAD_CHUNKS):
        part = slice(chunk * chunk_width, (chunk + 1) * chunk_width)
        mine, theirs = attention(both_queries[:, :, part], query_bars, key_bars, rings[chunk])
        merged = merge(mine, swap_cores(theirs, tracks))
        attended[0].append(merged)
        for s in shifts:
            attended[s].append(shifted(merged, "head", head_parts, s))

    experts = tracks
    wide_router = jnp.pad(router, ((0, 0), (0, LANES - experts)))
    gain = norm_gain.reshape(1, width)
    hidden, stat = project(attended, out_weights, residual_in[0], gain, wide_router, experts)
    stats = [stat] + [shifted(stat, "head", head_parts, s) for s in shifts]

    capacity = 2 * events * TOP // experts
    chunks = max(1, min(SLOT_CHUNKS, capacity // 16))
    slots = capacity // chunks
    rows = experts * slots
    route = expert_route[0]
    flat = route.reshape(-1)
    hits = (flat[:, None] == jnp.arange(experts, dtype=jnp.int32)).astype(jnp.int32)
    rank = jnp.sum((jnp.cumsum(hits, axis=0) - hits) * hits, axis=1)
    code = (rank // slots * rows + flat * slots + rank % slots).reshape(events, TOP)
    *outgoing, gates = pack(hidden, stats, gain, route, code.T, chunks, rows, experts)

    returned = []
    for chunk in range(chunks):
        arrived = lax.all_to_all(
            outgoing[chunk].reshape(experts, slots, width), "track", 0, 0, tiled=True
        ).reshape(rows, width)
        arrived = [arrived] + [shifted(arrived, "head", head_parts, s) for s in shifts]
        act = expert_in(arrived, w_gate, w_up, my_head)
        acts = [act] + [shifted(act, "head", head_parts, s) for s in shifts]
        result = expert_out(acts, down_weights)
        back = lax.all_to_all(result.reshape(experts, slots, width), "track", 0, 0, tiled=True)
        returned.append(back.reshape(rows, width))
    return combine(hidden, gates, code, returned)[None]


def solution(mesh):
    chips, columns = mesh.shape["track"] // 2, mesh.shape["head"]
    order = chip_ring(chips // columns, columns)
    in_specs = (
        P("track", None, "head"),
        P("track", None, "head"),
        P("track", None, "head"),
        P("track", None, "head"),
        P(),
        P(),
        P("head", None),
        P("head"),
        P("head", None),
        P("track", None, None),
        P("track", None, "head"),
        P("track", None, "head"),
        P("track", "head", None),
    )
    out_specs = P("track", None, "head")
    return jax.shard_map(
        functools.partial(local, order),
        mesh=mesh,
        in_specs=in_specs,
        out_specs=out_specs,
        check_vma=False,
    )
```

```python
import functools
import math

import jax
import jax.numpy as jnp
from jax import lax
from jax.experimental import pallas as pl
from jax.experimental.pallas import tpu as pltpu
from jax.sharding import PartitionSpec as P

D = 2048
QB = 16
PAIRS = 4
BAND = 2
TOP = 2
HEAD_DIM = 128
FIRST_HEADS = 4
EXPERT_GROUPS = (3, 5, 7, 8)
TAG_ROWS = 16
LANES = 128

MASKED_SCORE = -1e30
NO_CAP = 3e38
NORM_EPSILON = 1e-06
F32 = jnp.float32
BF16 = jnp.bfloat16


def dot(a, b):
    return jnp.dot(a, b, preferred_element_type=F32)


def dot_nt(a, b):
    return lax.dot_general(a, b, (((1,), (1,)), ((), ())), preferred_element_type=F32)


def chip_ring(rows, columns):
    order = []
    for row in range(rows):
        inner = list(range(1, columns))
        order += [(row, x) for x in (inner if row % 2 == 0 else inner[::-1])]
    order += [(row, 0) for row in range(rows - 1, -1, -1)]
    return [z * columns + x for z, x in order]


def shifted(x, axis, size, shift):
    return lax.ppermute(x, axis, [(i, (i + shift) % size) for i in range(size)])


def swap_cores(x, tracks):
    return lax.ppermute(x, "track", [(i, i ^ 1) for i in range(tracks)])


def attention_kernel(blocks, heads, causal, carried, *refs):
    q_ref, qbar_ref, kbar_ref = refs[:3]
    kv_refs = refs[3 : 3 + blocks]
    earlier = refs[3 + blocks : 3 + blocks + 2 * carried]
    *out_refs, cap_ref, score_ref = refs[3 + blocks + 2 * carried :]
    head = pl.program_id(0)
    events = q_ref.shape[1]
    exponent_scale = math.log2(math.e) / math.sqrt(HEAD_DIM)

    @pl.when(head == 0)
    def _():
        row = lax.broadcasted_iota(jnp.int32, (events, events), 0)
        column = lax.broadcasted_iota(jnp.int32, (events, events), 1)
        for side in range(2):
            for b in range(blocks):
                back = qbar_ref[side, :, b : b + 1] - kbar_ref[b : b + 1, :]
                allowed = (back >= 0) & (back <= BAND)
                if causal and side == 0 and b == 0:
                    allowed = allowed & (column <= row)
                cap_ref[b, side] = jnp.where(allowed, NO_CAP, MASKED_SCORE)

    lane = lax.broadcasted_iota(jnp.int32, (events, LANES), 1)
    columns = pl.ds(pl.multiple_of(head * HEAD_DIM, HEAD_DIM), HEAD_DIM)
    for side, out_ref in enumerate(out_refs):
        query = q_ref[side]
        peaks = None
        for b in range(blocks):
            scores = jnp.minimum(dot_nt(query, kv_refs[b][0]), cap_ref[b, side])
            score_ref[b] = scores
            for start in range(0, events, LANES):
                part = scores[:, start : start + LANES]
                peaks = part if peaks is None else jnp.maximum(peaks, part)
        peak = peaks.max(axis=1, keepdims=True)
        value = jnp.zeros((events, HEAD_DIM), F32)
        mass = jnp.zeros((events, 1), F32)
        if carried:
            stat = earlier[side][:, heads * HEAD_DIM :]
            old_peak = jnp.sum(jnp.where(lane == head, stat, 0.0), axis=1, keepdims=True)
            mass = jnp.sum(jnp.where(lane == heads + head, stat, 0.0), axis=1, keepdims=True)
            peak = jnp.maximum(peak, old_peak)
            shrink = jnp.exp2((old_peak - peak) * exponent_scale)
            mass = mass * shrink
            value = earlier[side][:, columns] * shrink
        masses = jnp.zeros((events, LANES), F32)
        for b in range(blocks):
            weights = jnp.exp2((score_ref[b] - peak) * exponent_scale)
            for start in range(0, events, LANES):
                masses = masses + weights[:, start : start + LANES]
            value = value + dot(weights.astype(BF16), kv_refs[b][1])
        mass = mass + masses.sum(axis=1, keepdims=True)
        out_ref[:, columns] = value
        stat = jnp.where(lane == head, peak, jnp.where(lane == heads + head, mass, 0.0))

        @pl.when(head == 0)
        def _():
            out_ref[:, heads * HEAD_DIM :] = stat

        @pl.when(head != 0)
        def _():
            out_ref[:, heads * HEAD_DIM :] += stat


def attention(q, qbar, kbar, kvs, causal, earlier=()):
    blocks, events, width = len(kvs), q.shape[1], q.shape[2]
    heads = width // HEAD_DIM
    shape = jax.ShapeDtypeStruct((events, width + LANES), F32)
    flops = 4 * 2 * events * blocks * events * width
    return pl.pallas_call(
        functools.partial(attention_kernel, blocks, heads, causal, bool(earlier)),
        grid=(heads,),
        in_specs=[
            pl.BlockSpec((2, events, HEAD_DIM), lambda h: (0, 0, h)),
            pl.BlockSpec(qbar.shape, lambda h: (0, 0, 0)),
            pl.BlockSpec(kbar.shape, lambda h: (0, 0)),
        ]
        + [pl.BlockSpec((2, events, HEAD_DIM), lambda h: (0, 0, h))] * blocks
        + [pl.BlockSpec(shape.shape, lambda h: (0, 0))] * len(earlier),
        out_specs=[pl.BlockSpec(shape.shape, lambda h: (0, 0))] * 2,
        out_shape=[shape, shape],
        scratch_shapes=[
            pltpu.VMEM((blocks, 2, events, events), F32),
            pltpu.VMEM((blocks, events, events), F32),
        ],
        cost_estimate=pl.CostEstimate(
            flops=flops, bytes_accessed=blocks * events * width * 4, transcendentals=flops // 512
        ),
        name="attention",
    )(q, qbar, kbar, *kvs, *earlier)


def merge_kernel(heads, a_ref, b_ref, out_ref):
    scale = 1.0 / math.sqrt(HEAD_DIM)
    for head in range(heads):
        at = heads * HEAD_DIM + head
        peak_a, mass_a = a_ref[:, at : at + 1], a_ref[:, at + heads : at + heads + 1]
        peak_b, mass_b = b_ref[:, at : at + 1], b_ref[:, at + heads : at + heads + 1]
        peak = jnp.maximum(peak_a, peak_b)
        scale_a = jnp.exp((peak_a - peak) * scale)
        scale_b = jnp.exp((peak_b - peak) * scale)
        part = slice(head * HEAD_DIM, (head + 1) * HEAD_DIM)
        total = scale_a * a_ref[:, part] + scale_b * b_ref[:, part]
        out_ref[:, part] = (total / (scale_a * mass_a + scale_b * mass_b)).astype(BF16)


def merge(a, b):
    events, width = a.shape[0], a.shape[1] - LANES
    return pl.pallas_call(
        functools.partial(merge_kernel, width // HEAD_DIM),
        out_shape=jax.ShapeDtypeStruct((events, width), BF16),
        cost_estimate=pl.CostEstimate(
            flops=8 * events * width, bytes_accessed=10 * events * width, transcendentals=0
        ),
        name="merge",
    )(a, b)


def project_kernel(count, experts, *refs):
    attended, weights = refs[:count], refs[count : 2 * count]
    residual_ref, gain_ref, router_ref, hidden_ref, stat_ref = refs[2 * count :]
    step = pl.program_id(0)
    total = residual_ref[...].astype(F32)
    for part, weight in zip(attended, weights, strict=True):
        total = total + dot(part[...], weight[...])
    hidden = total.astype(BF16)
    hidden_ref[...] = hidden
    wide = hidden.astype(F32)
    scaled = (wide * gain_ref[...].astype(F32)).astype(BF16)
    lane = lax.broadcasted_iota(jnp.int32, stat_ref.shape, 1)
    square = jnp.sum(wide * wide, axis=1, keepdims=True)
    stat = dot(scaled, router_ref[...]) + jnp.where(lane == experts, square, 0.0)

    @pl.when(step == 0)
    def _():
        stat_ref[...] = stat

    @pl.when(step != 0)
    def _():
        stat_ref[...] += stat


def project(attended, weights, residual, gain, router, experts):
    events, width = residual.shape
    tile = 256
    return pl.pallas_call(
        functools.partial(project_kernel, len(attended), experts),
        grid=(width // tile,),
        in_specs=[pl.BlockSpec(part.shape, lambda j: (0, 0)) for part in attended]
        + [pl.BlockSpec((w.shape[0], tile), lambda j: (0, j)) for w in weights]
        + [
            pl.BlockSpec((events, tile), lambda j: (0, j)),
            pl.BlockSpec((1, tile), lambda j: (0, j)),
            pl.BlockSpec((tile, LANES), lambda j: (j, 0)),
        ],
        out_specs=[
            pl.BlockSpec((events, tile), lambda j: (0, j)),
            pl.BlockSpec((events, LANES), lambda j: (0, 0)),
        ],
        out_shape=[
            jax.ShapeDtypeStruct((events, width), BF16),
            jax.ShapeDtypeStruct((events, LANES), F32),
        ],
        cost_estimate=pl.CostEstimate(
            flops=2 * events * D * width, bytes_accessed=2 * D * width, transcendentals=0
        ),
        name="project",
    )(*attended, *weights, residual, gain, router)


def pack_kernel(sources, experts, *refs):
    hidden_ref = refs[0]
    stats = refs[1 : 1 + sources]
    gain_ref, route_ref, tag_ref, block_ref, gate_ref = refs[1 + sources :]
    total = functools.reduce(jnp.add, [s[...] for s in stats])
    events = total.shape[0]
    lane = lax.broadcasted_iota(jnp.int32, total.shape, 1)
    square = jnp.sum(jnp.where(lane == experts, total, 0.0), axis=1, keepdims=True)
    inverse = lax.rsqrt(square / D + NORM_EPSILON)
    block_ref[:events, :] = (
        hidden_ref[...].astype(F32) * inverse * gain_ref[...].astype(F32)
    ).astype(BF16)
    block_ref[events:, :events] = tag_ref[...]
    logits = total * inverse
    parts = []
    for k in range(TOP):
        chosen = jnp.sum(
            jnp.where(lane == route_ref[:, k : k + 1], logits, 0.0), axis=1, keepdims=True
        )
        parts.append(1.0 / (1.0 + jnp.exp(-chosen)))
    whole = parts[0] + parts[1]
    gate_ref[...] = jnp.where(
        lane == 0, parts[0] / whole, jnp.where(lane == 1, parts[1] / whole, 0.0)
    )


def pack(hidden, stats, gain, route, tags, experts):
    events, width = hidden.shape
    return pl.pallas_call(
        functools.partial(pack_kernel, len(stats), experts),
        out_shape=[
            jax.ShapeDtypeStruct((events + TAG_ROWS, width), BF16),
            jax.ShapeDtypeStruct((events, LANES), F32),
        ],
        cost_estimate=pl.CostEstimate(
            flops=8 * events * width, bytes_accessed=4 * events * width, transcendentals=0
        ),
        name="pack",
    )(hidden, *stats, gain, route, tags)


def select_kernel(count, slots, experts_ref, *refs):
    blocks, out_ref = refs[:count], refs[count]
    events = blocks[0].shape[0] - TAG_ROWS
    row = lax.broadcasted_iota(jnp.int32, (2 * slots, events), 0)
    expert = jnp.where(row < slots, experts_ref[0], experts_ref[1])
    wanted = (expert * slots + row % slots).astype(F32)
    for i, block in enumerate(blocks):
        tags = block[events:, :events].astype(F32)
        hit = wanted == tags[0:1, :] * slots + tags[1:2, :]
        for k in range(1, TOP):
            hit = hit | (wanted == tags[2 * k : 2 * k + 1, :] * slots + tags[2 * k + 1 : 2 * k + 2, :])
        rows = dot(jnp.where(hit, 1.0, 0.0).astype(BF16), block[:events, :]).astype(BF16)
        for e in range(2):
            out_ref[e, i * slots : (i + 1) * slots, :] = rows[e * slots : (e + 1) * slots]


def select(experts, blocks, slots):
    count, width = len(blocks), blocks[0].shape[1]
    out = jax.ShapeDtypeStruct((2, count * slots, width), BF16)
    return pl.pallas_call(
        functools.partial(select_kernel, count, slots),
        in_specs=[pl.BlockSpec(memory_space=pltpu.SMEM)]
        + [pl.BlockSpec(memory_space=pltpu.VMEM)] * count,
        out_shape=out,
        cost_estimate=pl.CostEstimate(
            flops=4 * count * slots * blocks[0].shape[0] * width,
            bytes_accessed=2 * count * width * (blocks[0].shape[0] + 2 * slots),
            transcendentals=0,
        ),
        name="select",
    )(experts, *blocks)


def expert_in_kernel(sources, per_source, kmap_ref, *refs):
    rows = refs[:sources]
    weights = refs[sources : sources + 4]
    out_ref, gate_sum, up_sum = refs[sources + 4 :]
    step = pl.program_id(0)

    @pl.when(step == 0)
    def _():
        gate_sum[...] = jnp.zeros_like(gate_sum)
        up_sum[...] = jnp.zeros_like(up_sum)

    for source in range(sources):

        @pl.when(step // per_source == source)
        def _():
            for e in range(2):
                x = rows[source][e]
                gate_sum[e] += dot_nt(x, weights[2 * e][0])
                up_sum[e] += dot_nt(x, weights[2 * e + 1][0])

    @pl.when(step == pl.num_programs(0) - 1)
    def _():
        gate = gate_sum[...]
        out_ref[...] = (gate / (1.0 + jnp.exp(-gate)) * up_sum[...]).astype(BF16)


def expert_in(rows, weights, my_head):
    sources = len(rows)
    _, count, width = rows[0].shape
    units = weights[0].shape[1]
    tile = min(width, 1024)
    per_source = width // tile
    steps = sources * per_source
    number = jnp.arange(steps, dtype=jnp.int32)
    kmap = (my_head - number // per_source + sources) % sources * per_source + number % per_source

    def row_map(source):
        return lambda k, m: (0, 0, jnp.clip(k - source * per_source, 0, per_source - 1))

    weight = pl.BlockSpec((1, units, tile), lambda k, m: (0, 0, m[k]))
    return pl.pallas_call(
        functools.partial(expert_in_kernel, sources, per_source),
        grid_spec=pltpu.PrefetchScalarGridSpec(
            num_scalar_prefetch=1,
            grid=(steps,),
            in_specs=[pl.BlockSpec((2, count, tile), row_map(s)) for s in range(sources)]
            + [weight] * 4,
            out_specs=pl.BlockSpec((2, count, units), lambda k, m: (0, 0, 0)),
            scratch_shapes=[pltpu.VMEM((2, count, units), F32)] * 2,
        ),
        out_shape=jax.ShapeDtypeStruct((2, count, units), BF16),
        cost_estimate=pl.CostEstimate(
            flops=8 * count * D * units,
            bytes_accessed=8 * D * units,
            transcendentals=2 * count * units,
        ),
        name="expert_in",
    )(kmap, *rows, *weights)


def expert_out_kernel(sources, slots, *refs):
    acts = refs[:sources]
    weights = refs[sources : 3 * sources]
    outs = refs[3 * sources :]
    for e in range(2):
        total = dot(acts[0][e], weights[e * sources][...])
        for s in range(1, sources):
            total = total + dot(acts[s][e], weights[e * sources + s][...])
        total = total.astype(BF16)
        for i, out_ref in enumerate(outs):
            out_ref[e] = total[i * slots : (i + 1) * slots]


def expert_out(acts, weights, slots):
    sources = len(acts)
    _, count, units = acts[0].shape
    width = weights[0][0].shape[1]
    blocks = count // slots
    tile = min(width, 512)
    return pl.pallas_call(
        functools.partial(expert_out_kernel, sources, slots),
        grid=(width // tile,),
        in_specs=[pl.BlockSpec((2, count, units), lambda j: (0, 0, 0))] * sources
        + [pl.BlockSpec((units, tile), lambda j: (0, j))] * (2 * sources),
        out_specs=[pl.BlockSpec((2, slots, tile), lambda j: (0, 0, j))] * blocks,
        out_shape=[jax.ShapeDtypeStruct((2, slots, width), BF16)] * blocks,
        cost_estimate=pl.CostEstimate(
            flops=4 * sources * count * units * width,
            bytes_accessed=4 * sources * units * width,
            transcendentals=0,
        ),
        name="expert_out",
    )(*acts, *weights[0], *weights[1])


def combine_kernel(first, count, slots, base_ref, gate_ref, code_ref, *refs):
    returned, out_ref = refs[:count], refs[count]
    total = base_ref[...].astype(F32)
    events = total.shape[0]
    column = lax.broadcasted_iota(jnp.int32, (events, 2 * slots), 1)
    picked = [None] * TOP
    for i, block in enumerate(returned):
        back = block[...].reshape(2 * slots, block.shape[2])
        for k in range(TOP):
            hit = column + (first + i) * 2 * slots == code_ref[:, k : k + 1]
            part = dot(jnp.where(hit, 1.0, 0.0).astype(BF16), back)
            picked[k] = part if i == 0 else picked[k] + part
    for k in range(TOP):
        total = total + picked[k] * gate_ref[:, k : k + 1]
    out_ref[...] = total.astype(out_ref.dtype)


def combine(base, gates, codes, returned, first, dtype):
    events, width = base.shape
    count, slots = len(returned), returned[0].shape[1]
    return pl.pallas_call(
        functools.partial(combine_kernel, first, count, slots),
        out_shape=jax.ShapeDtypeStruct((events, width), dtype),
        cost_estimate=pl.CostEstimate(
            flops=8 * events * count * slots * width,
            bytes_accessed=4 * count * slots * width,
            transcendentals=0,
        ),
        name="combine",
    )(base, gates, codes, *returned)


def local(
    order,
    residual_in,
    queries,
    key_vectors,
    values,
    bar_index,
    pair_offset,
    out_proj,
    norm_gain,
    router,
    expert_route,
    w_gate,
    w_up,
    w_down,
):
    tracks = lax.axis_size("track")
    head_parts = lax.axis_size("head")
    my_track = lax.axis_index("track")
    my_head = lax.axis_index("head")
    events, width = queries.shape[1], queries.shape[2]
    chips = len(order)
    shifts = range(1, head_parts)

    barrier = lax.optimization_barrier

    forward = [
        (2 * order[i] + c, 2 * order[(i + 1) % chips] + c) for i in range(chips) for c in range(2)
    ]
    backward = [(b, a) for a, b in forward]
    hops = [0]
    for s in range(1, chips // 2):
        hops += [-s, s]
    hops.append(chips // 2)

    place = [0] * chips
    for i, chip in enumerate(order):
        place[chip] = i
    my_place = jnp.array(place, jnp.int32)[my_track // 2]
    block_chip = jnp.array(order, jnp.int32)[(my_place + jnp.array(hops, jnp.int32)) % chips]
    block_track = block_chip * 2 + my_track % 2
    key_bars = bar_index[block_track]
    query_track = jnp.stack([my_track, my_track ^ 1])
    query_bars = bar_index[query_track]
    partner = (query_track[:, None, None] + 1 + pair_offset[query_track]) % tracks
    listed = jnp.any(partner[:, :, :, None] == block_track, axis=2)
    listed = listed | (query_track[:, None, None] == block_track)
    listed = jnp.repeat(listed, QB, axis=1)
    query_bars = jnp.where(listed, query_bars[:, :, None], -1000)

    def columns_of(weight, owner):
        return lax.dynamic_slice_in_dim(weight, owner * width, width, 1)

    all_heads = width // HEAD_DIM
    cut = all_heads * FIRST_HEADS // 8 * HEAD_DIM
    parts = [slice(0, cut), slice(cut, width)]
    got = [
        [jnp.concatenate([key_vectors[:, :, part], values[:, :, part]], axis=0)] for part in parts
    ]
    both_queries = jnp.concatenate([queries, swap_cores(queries, tracks)], axis=0)
    chunk_queries = [both_queries[:, :, part] for part in parts]
    fetched = []
    for s in shifts:
        owner = (my_head + s) % head_parts
        out_part = columns_of(out_proj, owner)
        down_part = columns_of(w_down[0], owner)
        for part in (out_part[:cut], out_part[cut:], down_part):
            if fetched:
                part, fetched[-1] = barrier((part, fetched[-1]))
            fetched.append(shifted(part, "head", head_parts, s))
    in_weights = [jnp.swapaxes(w_gate, 1, 2), jnp.swapaxes(w_up, 1, 2)]
    in_weights += [swap_cores(w, tracks) for w in in_weights]

    steps = chips // 2
    ahead, back = [g[0] for g in got], [g[0] for g in got]
    for _ in range(1, steps):
        for i in range(2):
            ahead[i] = lax.ppermute(ahead[i], "track", forward)
            back[i] = lax.ppermute(back[i], "track", backward)
            got[i] += [ahead[i], back[i]]
    got[0].append(lax.ppermute(ahead[0], "track", forward))
    got[1].append(lax.ppermute(back[1], "track", backward))

    attended = [[] for _ in range(head_parts)]
    for i in range(2):
        mine, theirs = attention(chunk_queries[i], query_bars, key_bars, got[i], True)
        merged = merge(mine, swap_cores(theirs, tracks))
        attended[0].append(merged)
        for s in shifts:
            attended[s].append(shifted(merged, "head", head_parts, s))
    attended[0][0], fetched = barrier((attended[0][0], fetched))

    own_out = columns_of(out_proj, my_head)
    out_weights = [own_out[:cut], own_out[cut:]]
    down_weights = [columns_of(w_down[0], my_head)]
    for s in shifts:
        top, bottom, down = fetched[3 * s - 3 : 3 * s]
        out_weights += [top, bottom]
        down_weights.append(down)
    down_weights = [down_weights, [swap_cores(w, tracks) for w in down_weights]]

    experts = tracks
    wide_router = jnp.pad(router, ((0, 0), (0, LANES - experts)))
    gain = norm_gain.reshape(1, width)
    attended = [part for source in attended for part in source]
    hidden, stat = project(attended, out_weights, residual_in[0], gain, wide_router, experts)
    stats = [stat] + [shifted(stat, "head", head_parts, s) for s in shifts]

    slots = 2 * events * TOP // experts
    route = expert_route[0]
    flat = route.reshape(-1)
    hits = (flat[:, None] == jnp.arange(experts, dtype=jnp.int32)).astype(jnp.int32)
    rank = jnp.sum((jnp.cumsum(hits, axis=0) - hits) * hits, axis=1).reshape(events, TOP)
    tags = jnp.stack([route, rank], axis=2).reshape(events, 2 * TOP).T.astype(BF16)
    tags = jnp.pad(tags, ((0, TAG_ROWS - 2 * TOP), (0, 0)))
    hop_number = [0] * chips
    for i, hop in enumerate(hops):
        hop_number[hop % chips] = i
    hop_of_chip = jnp.array(hop_number, jnp.int32)[(my_place - jnp.array(place, jnp.int32)) % chips]
    chip_match = (route // 2)[:, :, None] == jnp.arange(chips, dtype=jnp.int32)
    hop_of_route = jnp.sum(jnp.where(chip_match, hop_of_chip, 0), axis=2)
    other_core = (route % 2 != my_track % 2).astype(jnp.int32)
    codes = (hop_of_route * 2 + other_core) * slots + rank
    my_experts = jnp.stack([my_track, my_track ^ 1])

    block, gates = pack(hidden, stats, gain, route, tags, experts)
    ends = [chips * share // 8 for share in EXPERT_GROUPS]
    blocks, forth, back = [block], block, block
    picked, ready = [], []
    for step in range(1, chips // 2 + 1):
        for group, when in enumerate(ready):
            if when == step - 2:
                forth, back, picked[group] = barrier((forth, back, picked[group]))
        forth = lax.ppermute(forth, "track", forward)
        blocks.append(forth)
        if step < chips // 2:
            back = lax.ppermute(back, "track", backward)
            blocks.append(back)
        while len(picked) < len(ends) and len(blocks) >= ends[len(picked)]:
            first = ends[len(picked) - 1] if picked else 0
            picked.append(select(my_experts, blocks[first : ends[len(picked)]], slots))
            ready.append(step)

    def across(x):
        return [x] + [shifted(x, "head", head_parts, s) for s in shifts]

    acts, returned, waiting, first = [], [], None, 0
    starts = [0] + ends[:-1]
    for group in range(len(ends) + 1):
        if group < len(ends):
            rows = across(picked[group])
            if waiting is not None:
                rows, waiting = barrier((rows, waiting))
            acts.append(across(expert_in(rows, in_weights, my_head)))
        if group > 0:
            outs = expert_out(acts[group - 1], down_weights, slots)
            for i, out in enumerate(outs):
                hop_length = hops[starts[group - 1] + i]
                pairs = [
                    (2 * order[p] + c, 2 * order[(p + hop_length) % chips] + c)
                    for p in range(chips)
                    for c in range(2)
                ]
                returned.append(lax.ppermute(out, "track", pairs) if hop_length else out)
            waiting = outs[0]
    result = combine(hidden, gates, codes, returned[: starts[-1]], 0, F32)
    result = combine(result, gates, codes, returned[starts[-1] :], starts[-1], BF16)
    return result[None]


def solution(mesh):
    chips, columns = mesh.shape["track"] // 2, mesh.shape["head"]
    order = chip_ring(chips // columns, columns)
    in_specs = (
        P("track", None, "head"),
        P("track", None, "head"),
        P("track", None, "head"),
        P("track", None, "head"),
        P(),
        P(),
        P("head", None),
        P("head"),
        P("head", None),
        P("track", None, None),
        P("track", None, "head"),
        P("track", None, "head"),
        P("track", "head", None),
    )
    out_specs = P("track", None, "head")
    return jax.shard_map(
        functools.partial(local, order),
        mesh=mesh,
        in_specs=in_specs,
        out_specs=out_specs,
        check_vma=False,
    )
```

```python
import functools
import math

import jax
import jax.numpy as jnp
from jax import lax
from jax.experimental import pallas as pl
from jax.experimental.pallas import tpu as pltpu
from jax.sharding import PartitionSpec as P

D = 2048
QB = 16
PAIRS = 4
BAND = 2
TOP = 2
HEAD_DIM = 128
EXPERT_GROUPS = (3, 5, 7, 8)
TAG_ROWS = 16
LANES = 128

MASKED_SCORE = -1e30
NO_CAP = 3e38
NORM_EPSILON = 1e-06
F32 = jnp.float32
BF16 = jnp.bfloat16


def dot(a, b):
    return jnp.dot(a, b, preferred_element_type=F32)


def dot_nt(a, b):
    return lax.dot_general(a, b, (((1,), (1,)), ((), ())), preferred_element_type=F32)


def chip_ring(rows, columns):
    order = []
    for row in range(rows):
        inner = list(range(1, columns))
        order += [(row, x) for x in (inner if row % 2 == 0 else inner[::-1])]
    order += [(row, 0) for row in range(rows - 1, -1, -1)]
    return [z * columns + x for z, x in order]


def shifted(x, axis, size, shift):
    return lax.ppermute(x, axis, [(i, (i + shift) % size) for i in range(size)])


def swap_cores(x, tracks):
    return lax.ppermute(x, "track", [(i, i ^ 1) for i in range(tracks)])


def halves_kernel(count, which_ref, *refs):
    for i in range(2):
        for j in range(count):
            refs[2 * count + i][j] = refs[i * count + j][0]


def halves(core, *arrays):
    _, events, width = arrays[0].shape
    count = len(arrays)
    block = (1, events, width // 2)
    shape = jax.ShapeDtypeStruct((count, events, width // 2), BF16)
    return pl.pallas_call(
        functools.partial(halves_kernel, count),
        grid_spec=pltpu.PrefetchScalarGridSpec(
            num_scalar_prefetch=1,
            grid=(1,),
            in_specs=[pl.BlockSpec(block, lambda g, m: (0, 0, m[0]))] * count
            + [pl.BlockSpec(block, lambda g, m: (0, 0, m[1]))] * count,
            out_specs=[pl.BlockSpec(shape.shape, lambda g, m: (0, 0, 0))] * 2,
        ),
        out_shape=[shape, shape],
        compiler_params=pltpu.CompilerParams(vmem_limit_bytes=16 << 20),
        cost_estimate=pl.CostEstimate(
            flops=0, bytes_accessed=4 * count * events * width, transcendentals=0
        ),
        name="halves",
    )(jnp.stack([core, 1 - core]), *arrays, *arrays)


def attention_kernel(blocks, *refs):
    q_ref, qbar_ref, kbar_ref = refs[:3]
    kv_refs = refs[3 : 3 + blocks]
    *out_refs, cap_ref, score_ref = refs[3 + blocks :]
    events = q_ref.shape[1]
    exponent_scale = math.log2(math.e) / math.sqrt(HEAD_DIM)

    @pl.when(pl.program_id(0) == 0)
    def _():
        row = lax.broadcasted_iota(jnp.int32, (events, events), 0)
        column = lax.broadcasted_iota(jnp.int32, (events, events), 1)
        for side in range(2):
            for b in range(blocks):
                back = qbar_ref[side, :, b : b + 1] - kbar_ref[b : b + 1, :]
                allowed = (back >= 0) & (back <= BAND)
                if side == b:
                    allowed = allowed & (column <= row)
                cap_ref[b, side] = jnp.where(allowed, NO_CAP, MASKED_SCORE).astype(cap_ref.dtype)

    for side, out_ref in enumerate(out_refs):
        query = q_ref[side]
        peaks = None
        for b in range(blocks):
            scores = jnp.minimum(dot_nt(query, kv_refs[b][0]), cap_ref[b, side].astype(F32))
            score_ref[b] = scores
            for start in range(0, events, LANES):
                part = scores[:, start : start + LANES]
                peaks = part if peaks is None else jnp.maximum(peaks, part)
        peak = peaks.max(axis=1, keepdims=True)
        value = jnp.zeros((events, HEAD_DIM), F32)
        masses = jnp.zeros((events, LANES), F32)
        for b in range(blocks):
            weights = jnp.exp2((score_ref[b] - peak) * exponent_scale)
            for start in range(0, events, LANES):
                masses = masses + weights[:, start : start + LANES]
            value = value + dot(weights.astype(BF16), kv_refs[b][1])
        out_ref[...] = (value / masses.sum(axis=1, keepdims=True)).astype(BF16)


def attention(q, qbar, kbar, kvs, first, heads):
    blocks, events = len(kvs), q.shape[1]
    shape = jax.ShapeDtypeStruct((events, heads * HEAD_DIM), BF16)
    flops = 4 * 2 * events * blocks * events * heads * HEAD_DIM
    part = pl.BlockSpec((2, events, HEAD_DIM), lambda h: (0, 0, first + h))
    return pl.pallas_call(
        functools.partial(attention_kernel, blocks),
        grid=(heads,),
        in_specs=[
            part,
            pl.BlockSpec(qbar.shape, lambda h: (0, 0, 0)),
            pl.BlockSpec(kbar.shape, lambda h: (0, 0)),
        ]
        + [part] * blocks,
        out_specs=[pl.BlockSpec((events, HEAD_DIM), lambda h: (0, h))] * 2,
        out_shape=[shape, shape],
        scratch_shapes=[
            pltpu.VMEM((blocks, 2, events, events), F32 if blocks <= 16 else BF16),
            pltpu.VMEM((blocks, events, events), F32),
        ],
        cost_estimate=pl.CostEstimate(
            flops=flops,
            bytes_accessed=4 * blocks * events * heads * HEAD_DIM,
            transcendentals=flops // 512,
        ),
        compiler_params=pltpu.CompilerParams(
            vmem_limit_bytes=(28 if blocks <= 16 else 60) << 20
        ),
        name="attention",
    )(q, qbar, kbar, *kvs)


def project_kernel(count, experts, place_ref, *refs):
    attended, weights = refs[:count], refs[count : 2 * count]
    residual_ref, gain_ref, router_ref, hidden_ref, stat_ref = refs[2 * count :]
    step = pl.program_id(0)
    total = residual_ref[...].astype(F32)
    for part, weight in zip(attended, weights, strict=True):
        total = total + dot(part[...], weight[...])
    hidden = total.astype(BF16)
    hidden_ref[...] = hidden
    wide = hidden.astype(F32)
    scaled = (wide * gain_ref[...].astype(F32)).astype(BF16)
    lane = lax.broadcasted_iota(jnp.int32, stat_ref.shape, 1)
    square = jnp.sum(wide * wide, axis=1, keepdims=True)
    stat = dot(scaled, router_ref[...]) + jnp.where(lane == experts, square, 0.0)

    @pl.when(step == 0)
    def _():
        stat_ref[...] = stat

    @pl.when(step != 0)
    def _():
        stat_ref[...] += stat


def project(attended, weights, places, residual, gain, router, experts):
    events, width = residual.shape
    tile = 256
    return pl.pallas_call(
        functools.partial(project_kernel, len(attended), experts),
        grid_spec=pltpu.PrefetchScalarGridSpec(
            num_scalar_prefetch=1,
            grid=(width // tile,),
            in_specs=[pl.BlockSpec(part.shape, lambda j, m: (0, 0)) for part in attended]
            + [
                pl.BlockSpec((part.shape[1], tile), lambda j, m, i=i: (m[i], j))
                for i, part in enumerate(attended)
            ]
            + [
                pl.BlockSpec((events, tile), lambda j, m: (0, j)),
                pl.BlockSpec((1, tile), lambda j, m: (0, j)),
                pl.BlockSpec((tile, LANES), lambda j, m: (j, 0)),
            ],
            out_specs=[
                pl.BlockSpec((events, tile), lambda j, m: (0, j)),
                pl.BlockSpec((events, LANES), lambda j, m: (0, 0)),
            ],
        ),
        out_shape=[
            jax.ShapeDtypeStruct((events, width), BF16),
            jax.ShapeDtypeStruct((events, LANES), F32),
        ],
        cost_estimate=pl.CostEstimate(
            flops=2 * events * D * width, bytes_accessed=2 * D * width, transcendentals=0
        ),
        compiler_params=pltpu.CompilerParams(vmem_limit_bytes=24 << 20),
        name="project",
    )(places, *attended, *weights, residual, gain, router)


def pack_kernel(sources, experts, *refs):
    hidden_ref = refs[0]
    stats = refs[1 : 1 + sources]
    gain_ref, route_ref, tag_ref, block_ref, gate_ref = refs[1 + sources :]
    total = functools.reduce(jnp.add, [s[...] for s in stats])
    events = total.shape[0]
    lane = lax.broadcasted_iota(jnp.int32, total.shape, 1)
    square = jnp.sum(jnp.where(lane == experts, total, 0.0), axis=1, keepdims=True)
    inverse = lax.rsqrt(square / D + NORM_EPSILON)
    block_ref[:events, :] = (
        hidden_ref[...].astype(F32) * inverse * gain_ref[...].astype(F32)
    ).astype(BF16)
    block_ref[events:, :events] = tag_ref[...]
    logits = total * inverse
    parts = []
    for k in range(TOP):
        chosen = jnp.sum(
            jnp.where(lane == route_ref[:, k : k + 1], logits, 0.0), axis=1, keepdims=True
        )
        parts.append(1.0 / (1.0 + jnp.exp(-chosen)))
    whole = parts[0] + parts[1]
    gate_ref[...] = jnp.where(
        lane == 0, parts[0] / whole, jnp.where(lane == 1, parts[1] / whole, 0.0)
    )


def pack(hidden, stats, gain, route, tags, experts):
    events, width = hidden.shape
    return pl.pallas_call(
        functools.partial(pack_kernel, len(stats), experts),
        out_shape=[
            jax.ShapeDtypeStruct((events + TAG_ROWS, width), BF16),
            jax.ShapeDtypeStruct((events, LANES), F32),
        ],
        cost_estimate=pl.CostEstimate(
            flops=8 * events * width, bytes_accessed=4 * events * width, transcendentals=0
        ),
        compiler_params=pltpu.CompilerParams(vmem_limit_bytes=16 << 20),
        name="pack",
    )(hidden, *stats, gain, route, tags)


def select_kernel(count, slots, experts_ref, *refs):
    blocks, out_ref = refs[:count], refs[count]
    events = blocks[0].shape[0] - TAG_ROWS
    row = lax.broadcasted_iota(jnp.int32, (2 * slots, events), 0)
    expert = jnp.where(row < slots, experts_ref[0], experts_ref[1])
    wanted = (expert * slots + row % slots).astype(F32)
    for i, block in enumerate(blocks):
        tags = block[events:, :events].astype(F32)
        hit = wanted == tags[0:1, :] * slots + tags[1:2, :]
        for k in range(1, TOP):
            hit = hit | (wanted == tags[2 * k : 2 * k + 1, :] * slots + tags[2 * k + 1 : 2 * k + 2, :])
        rows = dot(jnp.where(hit, 1.0, 0.0).astype(BF16), block[:events, :]).astype(BF16)
        for e in range(2):
            out_ref[e, i * slots : (i + 1) * slots, :] = rows[e * slots : (e + 1) * slots]


def select(experts, blocks, slots):
    count, width = len(blocks), blocks[0].shape[1]
    out = jax.ShapeDtypeStruct((2, count * slots, width), BF16)
    return pl.pallas_call(
        functools.partial(select_kernel, count, slots),
        in_specs=[pl.BlockSpec(memory_space=pltpu.SMEM)]
        + [pl.BlockSpec(memory_space=pltpu.VMEM)] * count,
        out_shape=out,
        cost_estimate=pl.CostEstimate(
            flops=4 * count * slots * blocks[0].shape[0] * width,
            bytes_accessed=2 * count * width * (blocks[0].shape[0] + 2 * slots),
            transcendentals=0,
        ),
        compiler_params=pltpu.CompilerParams(vmem_limit_bytes=16 << 20),
        name="select",
    )(experts, *blocks)


def expert_in_kernel(sources, per_source, kmap_ref, *refs):
    rows = refs[:sources]
    weights = refs[sources : sources + 4]
    out_ref, gate_sum, up_sum = refs[sources + 4 :]
    step = pl.program_id(0)

    @pl.when(step == 0)
    def _():
        gate_sum[...] = jnp.zeros_like(gate_sum)
        up_sum[...] = jnp.zeros_like(up_sum)

    for source in range(sources):

        @pl.when(step // per_source == source)
        def _():
            for e in range(2):
                x = rows[source][e]
                gate_sum[e] += dot_nt(x, weights[2 * e][0])
                up_sum[e] += dot_nt(x, weights[2 * e + 1][0])

    @pl.when(step == pl.num_programs(0) - 1)
    def _():
        gate = gate_sum[...]
        out_ref[...] = (gate / (1.0 + jnp.exp(-gate)) * up_sum[...]).astype(BF16)


def expert_in(rows, weights, my_head):
    sources = len(rows)
    _, count, width = rows[0].shape
    units = weights[0].shape[1]
    tile = min(width, 1024)
    per_source = width // tile
    steps = sources * per_source
    number = jnp.arange(steps, dtype=jnp.int32)
    kmap = (my_head - number // per_source + sources) % sources * per_source + number % per_source

    def row_map(source):
        return lambda k, m: (0, 0, jnp.clip(k - source * per_source, 0, per_source - 1))

    weight = pl.BlockSpec((1, units, tile), lambda k, m: (0, 0, m[k]))
    return pl.pallas_call(
        functools.partial(expert_in_kernel, sources, per_source),
        grid_spec=pltpu.PrefetchScalarGridSpec(
            num_scalar_prefetch=1,
            grid=(steps,),
            in_specs=[pl.BlockSpec((2, count, tile), row_map(s)) for s in range(sources)]
            + [weight] * 4,
            out_specs=pl.BlockSpec((2, count, units), lambda k, m: (0, 0, 0)),
            scratch_shapes=[pltpu.VMEM((2, count, units), F32)] * 2,
        ),
        out_shape=jax.ShapeDtypeStruct((2, count, units), BF16),
        cost_estimate=pl.CostEstimate(
            flops=8 * count * D * units,
            bytes_accessed=8 * D * units,
            transcendentals=2 * count * units,
        ),
        compiler_params=pltpu.CompilerParams(vmem_limit_bytes=24 << 20),
        name="expert_in",
    )(kmap, *rows, *weights)


def expert_out_kernel(sources, slots, *refs):
    acts = refs[:sources]
    weights = refs[sources : 3 * sources]
    outs = refs[3 * sources :]
    for e in range(2):
        total = dot(acts[0][e], weights[e * sources][...])
        for s in range(1, sources):
            total = total + dot(acts[s][e], weights[e * sources + s][...])
        total = total.astype(BF16)
        for i, out_ref in enumerate(outs):
            out_ref[e] = total[i * slots : (i + 1) * slots]


def expert_out(acts, weights, slots):
    sources = len(acts)
    _, count, units = acts[0].shape
    width = weights[0][0].shape[1]
    blocks = count // slots
    tile = min(width, 512)
    return pl.pallas_call(
        functools.partial(expert_out_kernel, sources, slots),
        grid=(width // tile,),
        in_specs=[pl.BlockSpec((2, count, units), lambda j: (0, 0, 0))] * sources
        + [pl.BlockSpec((units, tile), lambda j: (0, j))] * (2 * sources),
        out_specs=[pl.BlockSpec((2, slots, tile), lambda j: (0, 0, j))] * blocks,
        out_shape=[jax.ShapeDtypeStruct((2, slots, width), BF16)] * blocks,
        cost_estimate=pl.CostEstimate(
            flops=4 * sources * count * units * width,
            bytes_accessed=4 * sources * units * width,
            transcendentals=0,
        ),
        compiler_params=pltpu.CompilerParams(vmem_limit_bytes=16 << 20),
        name="expert_out",
    )(*acts, *weights[0], *weights[1])


def combine_kernel(first, count, slots, base_ref, gate_ref, code_ref, *refs):
    returned, out_ref = refs[:count], refs[count]
    total = base_ref[...].astype(F32)
    events = total.shape[0]
    column = lax.broadcasted_iota(jnp.int32, (events, 2 * slots), 1)
    picked = [None] * TOP
    for i, block in enumerate(returned):
        back = block[...].reshape(2 * slots, block.shape[2])
        for k in range(TOP):
            hit = column + (first + i) * 2 * slots == code_ref[:, k : k + 1]
            part = dot(jnp.where(hit, 1.0, 0.0).astype(BF16), back)
            picked[k] = part if i == 0 else picked[k] + part
    for k in range(TOP):
        total = total + picked[k] * gate_ref[:, k : k + 1]
    out_ref[...] = total.astype(out_ref.dtype)


def combine(base, gates, codes, returned, first, dtype):
    events, width = base.shape
    count, slots = len(returned), returned[0].shape[1]
    return pl.pallas_call(
        functools.partial(combine_kernel, first, count, slots),
        out_shape=jax.ShapeDtypeStruct((events, width), dtype),
        cost_estimate=pl.CostEstimate(
            flops=8 * events * count * slots * width,
            bytes_accessed=4 * count * slots * width,
            transcendentals=0,
        ),
        compiler_params=pltpu.CompilerParams(vmem_limit_bytes=16 << 20),
        name="combine",
    )(base, gates, codes, *returned)


def local(
    order,
    residual_in,
    queries,
    key_vectors,
    values,
    bar_index,
    pair_offset,
    out_proj,
    norm_gain,
    router,
    expert_route,
    w_gate,
    w_up,
    w_down,
):
    tracks = lax.axis_size("track")
    head_parts = lax.axis_size("head")
    my_track = lax.axis_index("track")
    my_head = lax.axis_index("head")
    events, width = queries.shape[1], queries.shape[2]
    chips = len(order)
    shifts = range(1, head_parts)

    barrier = lax.optimization_barrier

    forward = [
        (2 * order[i] + c, 2 * order[(i + 1) % chips] + c) for i in range(chips) for c in range(2)
    ]
    backward = [(b, a) for a, b in forward]
    hops = [0]
    for s in range(1, chips // 2):
        hops += [-s, s]
    hops.append(chips // 2)

    place = [0] * chips
    for i, chip in enumerate(order):
        place[chip] = i
    my_place = jnp.array(place, jnp.int32)[my_track // 2]
    block_chip = jnp.array(order, jnp.int32)[(my_place + jnp.array(hops, jnp.int32)) % chips]
    core = my_track % 2
    block_track = jnp.stack([block_chip * 2 + core, block_chip * 2 + 1 - core], 1).reshape(-1)
    key_bars = bar_index[block_track]
    query_track = jnp.stack([my_track, my_track ^ 1])
    query_bars = bar_index[query_track]
    partner = (query_track[:, None, None] + 1 + pair_offset[query_track]) % tracks
    listed = jnp.any(partner[:, :, :, None] == block_track, axis=2)
    listed = listed | (query_track[:, None, None] == block_track)
    listed = jnp.repeat(listed, QB, axis=1)
    query_bars = jnp.where(listed, query_bars[:, :, None], -1000)

    def columns_of(weight, owner):
        return lax.dynamic_slice_in_dim(weight, owner * width, width, 1)

    own_half, other_half = halves(core, key_vectors, values)
    streams = [[own_half], [swap_cores(other_half, tracks)]]
    own_queries, other_queries = halves(core, queries)
    both_queries = jnp.concatenate([own_queries, swap_cores(other_queries, tracks)], axis=0)
    fetched = []
    for s in shifts:
        owner = (my_head + s) % head_parts
        for part in (columns_of(out_proj, owner), columns_of(w_down[0], owner)):
            if fetched:
                part, fetched[-1] = barrier((part, fetched[-1]))
            fetched.append(shifted(part, "head", head_parts, s))
    in_weights = [jnp.swapaxes(w_gate, 1, 2), jnp.swapaxes(w_up, 1, 2)]
    in_weights += [swap_cores(w, tracks) for w in in_weights]

    steps = chips // 2
    ahead, back = [g[0] for g in streams], [g[0] for g in streams]
    for _ in range(1, steps):
        for i in range(2):
            ahead[i] = lax.ppermute(ahead[i], "track", forward)
            back[i] = lax.ppermute(back[i], "track", backward)
            streams[i] += [ahead[i], back[i]]
    streams[0].append(lax.ppermute(ahead[0], "track", forward))
    streams[1].append(lax.ppermute(back[1], "track", backward))
    kvs = [block for pair in zip(*streams, strict=True) for block in pair]

    local_heads = width // HEAD_DIM // 2
    cuts = [0, local_heads - local_heads // 2, local_heads]
    attended, weight_of, places = [], [], []
    for first, end in zip(cuts[:-1], cuts[1:], strict=True):
        mine, theirs = attention(both_queries, query_bars, key_bars, kvs, first, end - first)
        pieces = [(0, 0, mine), (0, 1, swap_cores(theirs, tracks))]
        for s in shifts:
            pieces.append((s, 0, shifted(mine, "head", head_parts, s)))
            pairs = [
                (t * head_parts + h, (t ^ 1) * head_parts + (h + s) % head_parts)
                for t in range(tracks)
                for h in range(head_parts)
            ]
            pieces.append((s, 1, lax.ppermute(theirs, ("track", "head"), pairs)))
        for s, other, piece in pieces:
            attended.append(piece)
            weight_of.append(s)
            half = 1 - core if other else core
            places.append(half * (local_heads // (end - first)) + first // (end - first))
    attended[0], fetched = barrier((attended[0], fetched))
    out_weights = [columns_of(out_proj, my_head)] + fetched[::2]
    down_weights = [columns_of(w_down[0], my_head)]
    for s in shifts:
        down_weights.append(fetched[2 * s - 1])
    down_weights = [down_weights, [swap_cores(w, tracks) for w in down_weights]]

    experts = tracks
    wide_router = jnp.pad(router, ((0, 0), (0, LANES - experts)))
    gain = norm_gain.reshape(1, width)
    hidden, stat = project(
        attended,
        [out_weights[s] for s in weight_of],
        jnp.stack(places),
        residual_in[0],
        gain,
        wide_router,
        experts,
    )
    stats = [stat] + [shifted(stat, "head", head_parts, s) for s in shifts]

    slots = 2 * events * TOP // experts
    route = expert_route[0]
    flat = route.reshape(-1)
    hits = (flat[:, None] == jnp.arange(experts, dtype=jnp.int32)).astype(jnp.int32)
    rank = jnp.sum((jnp.cumsum(hits, axis=0) - hits) * hits, axis=1).reshape(events, TOP)
    tags = jnp.stack([route, rank], axis=2).reshape(events, 2 * TOP).T.astype(BF16)
    tags = jnp.pad(tags, ((0, TAG_ROWS - 2 * TOP), (0, 0)))
    hop_number = [0] * chips
    for i, hop in enumerate(hops):
        hop_number[hop % chips] = i
    hop_of_chip = jnp.array(hop_number, jnp.int32)[(my_place - jnp.array(place, jnp.int32)) % chips]
    chip_match = (route // 2)[:, :, None] == jnp.arange(chips, dtype=jnp.int32)
    hop_of_route = jnp.sum(jnp.where(chip_match, hop_of_chip, 0), axis=2)
    other_core = (route % 2 != my_track % 2).astype(jnp.int32)
    codes = (hop_of_route * 2 + other_core) * slots + rank
    my_experts = jnp.stack([my_track, my_track ^ 1])

    in_weights = [pltpu.with_memory_space_constraint(w, pltpu.VMEM) for w in in_weights]
    down_weights = [
        [pltpu.with_memory_space_constraint(w, pltpu.VMEM) for w in ws] for ws in down_weights
    ]
    block, gates = pack(hidden, stats, gain, route, tags, experts)
    ends = [chips * share // 8 for share in EXPERT_GROUPS]
    blocks, forth, back = [block], block, block
    picked, ready = [], []
    for step in range(1, chips // 2 + 1):
        for group, when in enumerate(ready):
            if when == step - 2:
                forth, back, picked[group] = barrier((forth, back, picked[group]))
        forth = lax.ppermute(forth, "track", forward)
        blocks.append(forth)
        if step < chips // 2:
            back = lax.ppermute(back, "track", backward)
            blocks.append(back)
        while len(picked) < len(ends) and len(blocks) >= ends[len(picked)]:
            first = ends[len(picked) - 1] if picked else 0
            picked.append(select(my_experts, blocks[first : ends[len(picked)]], slots))
            ready.append(step)

    def across(x):
        return [x] + [shifted(x, "head", head_parts, s) for s in shifts]

    acts, returned, waiting, first = [], [], None, 0
    starts = [0] + ends[:-1]
    for group in range(len(ends) + 1):
        if group < len(ends):
            rows = across(picked[group])
            if waiting is not None:
                rows, waiting = barrier((rows, waiting))
            acts.append(across(expert_in(rows, in_weights, my_head)))
        if group > 0:
            outs = expert_out(acts[group - 1], down_weights, slots)
            for i, out in enumerate(outs):
                hop_length = hops[starts[group - 1] + i]
                pairs = [
                    (2 * order[p] + c, 2 * order[(p + hop_length) % chips] + c)
                    for p in range(chips)
                    for c in range(2)
                ]
                returned.append(lax.ppermute(out, "track", pairs) if hop_length else out)
            waiting = outs[0]
    result = combine(hidden, gates, codes, returned[: starts[-1]], 0, F32)
    result = combine(result, gates, codes, returned[starts[-1] :], starts[-1], BF16)
    return result[None]


def solution(mesh):
    chips, columns = mesh.shape["track"] // 2, mesh.shape["head"]
    order = chip_ring(chips // columns, columns)
    in_specs = (
        P("track", None, "head"),
        P("track", None, "head"),
        P("track", None, "head"),
        P("track", None, "head"),
        P(),
        P(),
        P("head", None),
        P("head"),
        P("head", None),
        P("track", None, None),
        P("track", None, "head"),
        P("track", None, "head"),
        P("track", "head", None),
    )
    out_specs = P("track", None, "head")
    return jax.shard_map(
        functools.partial(local, order),
        mesh=mesh,
        in_specs=in_specs,
        out_specs=out_specs,
        check_vma=False,
    )
```

```python
import functools
import math

import jax
import jax.numpy as jnp
from jax import lax
from jax.experimental import pallas as pl
from jax.experimental.pallas import tpu as pltpu
from jax.sharding import PartitionSpec as P

D = 2048
QB = 16
PAIRS = 4
BAND = 2
TOP = 2
HEAD_DIM = 128
EXPERT_GROUPS = (3, 5, 7, 8)
TAG_ROWS = 16
LANES = 128

MASKED_SCORE = -1e30
NO_CAP = 3e38
NORM_EPSILON = 1e-06
F32 = jnp.float32
BF16 = jnp.bfloat16


def dot(a, b):
    return jnp.dot(a, b, preferred_element_type=F32)


def dot_nt(a, b):
    return lax.dot_general(a, b, (((1,), (1,)), ((), ())), preferred_element_type=F32)


def chip_ring(rows, columns):
    order = []
    for row in range(rows):
        inner = list(range(1, columns))
        order += [(row, x) for x in (inner if row % 2 == 0 else inner[::-1])]
    order += [(row, 0) for row in range(rows - 1, -1, -1)]
    return [z * columns + x for z, x in order]


def shifted(x, axis, size, shift):
    return lax.ppermute(x, axis, [(i, (i + shift) % size) for i in range(size)])


def swap_cores(x, tracks):
    return lax.ppermute(x, "track", [(i, i ^ 1) for i in range(tracks)])


def halves_kernel(count, which_ref, *refs):
    for i in range(2):
        for j in range(count):
            refs[2 * count + i][j] = refs[i * count + j][0]


def halves(core, *arrays):
    _, events, width = arrays[0].shape
    count = len(arrays)
    block = (1, events, width // 2)
    shape = jax.ShapeDtypeStruct((count, events, width // 2), BF16)
    return pl.pallas_call(
        functools.partial(halves_kernel, count),
        grid_spec=pltpu.PrefetchScalarGridSpec(
            num_scalar_prefetch=1,
            grid=(1,),
            in_specs=[pl.BlockSpec(block, lambda g, m: (0, 0, m[0]))] * count
            + [pl.BlockSpec(block, lambda g, m: (0, 0, m[1]))] * count,
            out_specs=[pl.BlockSpec(shape.shape, lambda g, m: (0, 0, 0))] * 2,
        ),
        out_shape=[shape, shape],
        compiler_params=pltpu.CompilerParams(vmem_limit_bytes=16 << 20),
        cost_estimate=pl.CostEstimate(
            flops=0, bytes_accessed=4 * count * events * width, transcendentals=0
        ),
        name="halves",
    )(jnp.stack([core, 1 - core]), *arrays, *arrays)


def attention_kernel(blocks, *refs):
    q_ref, qbar_ref, kbar_ref = refs[:3]
    kv_refs = refs[3 : 3 + blocks]
    *out_refs, cap_ref, score_ref = refs[3 + blocks :]
    events = q_ref.shape[1]
    exponent_scale = math.log2(math.e) / math.sqrt(HEAD_DIM)

    @pl.when(pl.program_id(0) == 0)
    def _():
        row = lax.broadcasted_iota(jnp.int32, (events, events), 0)
        column = lax.broadcasted_iota(jnp.int32, (events, events), 1)
        for side in range(2):
            for b in range(blocks):
                back = qbar_ref[side, :, b : b + 1] - kbar_ref[b : b + 1, :]
                allowed = (back >= 0) & (back <= BAND)
                if side == b:
                    allowed = allowed & (column <= row)
                cap_ref[b, side] = jnp.where(allowed, NO_CAP, MASKED_SCORE).astype(cap_ref.dtype)

    for side, out_ref in enumerate(out_refs):
        query = q_ref[side]
        peaks = None
        for b in range(blocks):
            scores = jnp.minimum(dot_nt(query, kv_refs[b][0]), cap_ref[b, side].astype(F32))
            score_ref[b] = scores
            for start in range(0, events, LANES):
                part = scores[:, start : start + LANES]
                peaks = part if peaks is None else jnp.maximum(peaks, part)
        peak = peaks.max(axis=1, keepdims=True)
        value = jnp.zeros((events, HEAD_DIM), F32)
        masses = jnp.zeros((events, LANES), F32)
        for b in range(blocks):
            weights = jnp.exp2((score_ref[b] - peak) * exponent_scale)
            for start in range(0, events, LANES):
                masses = masses + weights[:, start : start + LANES]
            value = value + dot(weights.astype(BF16), kv_refs[b][1])
        out_ref[...] = (value / masses.sum(axis=1, keepdims=True)).astype(BF16)


def attention(q, qbar, kbar, kvs, first, heads):
    blocks, events = len(kvs), q.shape[1]
    shape = jax.ShapeDtypeStruct((events, heads * HEAD_DIM), BF16)
    flops = 4 * 2 * events * blocks * events * heads * HEAD_DIM
    part = pl.BlockSpec((2, events, HEAD_DIM), lambda h: (0, 0, first + h))
    return pl.pallas_call(
        functools.partial(attention_kernel, blocks),
        grid=(heads,),
        in_specs=[
            part,
            pl.BlockSpec(qbar.shape, lambda h: (0, 0, 0)),
            pl.BlockSpec(kbar.shape, lambda h: (0, 0)),
        ]
        + [part] * blocks,
        out_specs=[pl.BlockSpec((events, HEAD_DIM), lambda h: (0, h))] * 2,
        out_shape=[shape, shape],
        scratch_shapes=[
            pltpu.VMEM((blocks, 2, events, events), F32 if blocks <= 16 else BF16),
            pltpu.VMEM((blocks, events, events), F32),
        ],
        cost_estimate=pl.CostEstimate(
            flops=flops,
            bytes_accessed=4 * blocks * events * heads * HEAD_DIM,
            transcendentals=flops // 512,
        ),
        compiler_params=pltpu.CompilerParams(
            vmem_limit_bytes=(28 if blocks <= 16 else 60) << 20
        ),
        name="attention",
    )(q, qbar, kbar, *kvs)


def project_kernel(count, experts, place_ref, *refs):
    attended, weights = refs[:count], refs[count : 2 * count]
    residual_ref, gain_ref, router_ref, hidden_ref, stat_ref = refs[2 * count :]
    step = pl.program_id(0)
    total = residual_ref[...].astype(F32)
    for part, weight in zip(attended, weights, strict=True):
        total = total + dot(part[...], weight[...])
    hidden = total.astype(BF16)
    hidden_ref[...] = hidden
    wide = hidden.astype(F32)
    scaled = (wide * gain_ref[...].astype(F32)).astype(BF16)
    lane = lax.broadcasted_iota(jnp.int32, stat_ref.shape, 1)
    square = jnp.sum(wide * wide, axis=1, keepdims=True)
    stat = dot(scaled, router_ref[...]) + jnp.where(lane == experts, square, 0.0)

    @pl.when(step == 0)
    def _():
        stat_ref[...] = stat

    @pl.when(step != 0)
    def _():
        stat_ref[...] += stat


def project(attended, weights, places, residual, gain, router, experts):
    events, width = residual.shape
    tile = 256
    count = len(attended)

    def weight_map(i):
        if weights[i].shape[1] > width:
            return lambda j, m: (m[i], m[count] + j)
        return lambda j, m: (m[i], j)

    return pl.pallas_call(
        functools.partial(project_kernel, len(attended), experts),
        grid_spec=pltpu.PrefetchScalarGridSpec(
            num_scalar_prefetch=1,
            grid=(width // tile,),
            in_specs=[pl.BlockSpec(part.shape, lambda j, m: (0, 0)) for part in attended]
            + [
                pl.BlockSpec(
                    (part.shape[1], tile),
                    weight_map(i),
                )
                for i, part in enumerate(attended)
            ]
            + [
                pl.BlockSpec((events, tile), lambda j, m: (0, j)),
                pl.BlockSpec((1, tile), lambda j, m: (0, j)),
                pl.BlockSpec((tile, LANES), lambda j, m: (j, 0)),
            ],
            out_specs=[
                pl.BlockSpec((events, tile), lambda j, m: (0, j)),
                pl.BlockSpec((events, LANES), lambda j, m: (0, 0)),
            ],
        ),
        out_shape=[
            jax.ShapeDtypeStruct((events, width), BF16),
            jax.ShapeDtypeStruct((events, LANES), F32),
        ],
        cost_estimate=pl.CostEstimate(
            flops=2 * events * D * width, bytes_accessed=2 * D * width, transcendentals=0
        ),
        compiler_params=pltpu.CompilerParams(vmem_limit_bytes=24 << 20),
        name="project",
    )(places, *attended, *weights, residual, gain, router)


def pack_kernel(sources, experts, *refs):
    hidden_ref = refs[0]
    stats = refs[1 : 1 + sources]
    gain_ref, route_ref, tag_ref, block_ref, gate_ref = refs[1 + sources :]
    total = functools.reduce(jnp.add, [s[...] for s in stats])
    events = total.shape[0]
    lane = lax.broadcasted_iota(jnp.int32, total.shape, 1)
    square = jnp.sum(jnp.where(lane == experts, total, 0.0), axis=1, keepdims=True)
    inverse = lax.rsqrt(square / D + NORM_EPSILON)
    block_ref[:events, :] = (
        hidden_ref[...].astype(F32) * inverse * gain_ref[...].astype(F32)
    ).astype(BF16)
    block_ref[events:, :events] = tag_ref[...]
    logits = total * inverse
    parts = []
    for k in range(TOP):
        chosen = jnp.sum(
            jnp.where(lane == route_ref[:, k : k + 1], logits, 0.0), axis=1, keepdims=True
        )
        parts.append(1.0 / (1.0 + jnp.exp(-chosen)))
    whole = parts[0] + parts[1]
    gate_ref[...] = jnp.where(
        lane == 0, parts[0] / whole, jnp.where(lane == 1, parts[1] / whole, 0.0)
    )


def pack(hidden, stats, gain, route, tags, experts):
    events, width = hidden.shape
    return pl.pallas_call(
        functools.partial(pack_kernel, len(stats), experts),
        out_shape=[
            jax.ShapeDtypeStruct((events + TAG_ROWS, width), BF16),
            jax.ShapeDtypeStruct((events, LANES), F32),
        ],
        cost_estimate=pl.CostEstimate(
            flops=8 * events * width, bytes_accessed=4 * events * width, transcendentals=0
        ),
        compiler_params=pltpu.CompilerParams(vmem_limit_bytes=16 << 20),
        name="pack",
    )(hidden, *stats, gain, route, tags)


def select_kernel(count, slots, experts_ref, *refs):
    blocks, out_ref = refs[:count], refs[count]
    events = blocks[0].shape[0] - TAG_ROWS
    row = lax.broadcasted_iota(jnp.int32, (2 * slots, events), 0)
    expert = jnp.where(row < slots, experts_ref[0], experts_ref[1])
    wanted = (expert * slots + row % slots).astype(F32)
    for i, block in enumerate(blocks):
        tags = block[events:, :events].astype(F32)
        hit = wanted == tags[0:1, :] * slots + tags[1:2, :]
        for k in range(1, TOP):
            hit = hit | (wanted == tags[2 * k : 2 * k + 1, :] * slots + tags[2 * k + 1 : 2 * k + 2, :])
        rows = dot(jnp.where(hit, 1.0, 0.0).astype(BF16), block[:events, :]).astype(BF16)
        for e in range(2):
            out_ref[e, i * slots : (i + 1) * slots, :] = rows[e * slots : (e + 1) * slots]


def select(experts, blocks, slots):
    count, width = len(blocks), blocks[0].shape[1]
    out = jax.ShapeDtypeStruct((2, count * slots, width), BF16)
    return pl.pallas_call(
        functools.partial(select_kernel, count, slots),
        in_specs=[pl.BlockSpec(memory_space=pltpu.SMEM)]
        + [pl.BlockSpec(memory_space=pltpu.VMEM)] * count,
        out_shape=out,
        cost_estimate=pl.CostEstimate(
            flops=4 * count * slots * blocks[0].shape[0] * width,
            bytes_accessed=2 * count * width * (blocks[0].shape[0] + 2 * slots),
            transcendentals=0,
        ),
        compiler_params=pltpu.CompilerParams(vmem_limit_bytes=16 << 20),
        name="select",
    )(experts, *blocks)


def expert_in_kernel(sources, per_source, kmap_ref, *refs):
    rows = refs[:sources]
    weights = refs[sources : sources + 4]
    out_ref, gate_sum, up_sum = refs[sources + 4 :]
    step = pl.program_id(0)

    @pl.when(step == 0)
    def _():
        gate_sum[...] = jnp.zeros_like(gate_sum)
        up_sum[...] = jnp.zeros_like(up_sum)

    for source in range(sources):

        @pl.when(step // per_source == source)
        def _():
            for e in range(2):
                x = rows[source][e]
                gate_sum[e] += dot_nt(x, weights[2 * e][0])
                up_sum[e] += dot_nt(x, weights[2 * e + 1][0])

    @pl.when(step == pl.num_programs(0) - 1)
    def _():
        gate = gate_sum[...]
        out_ref[...] = (gate / (1.0 + jnp.exp(-gate)) * up_sum[...]).astype(BF16)


def expert_in(rows, weights, my_head):
    sources = len(rows)
    _, count, width = rows[0].shape
    units = weights[0].shape[1]
    tile = min(width, 1024)
    per_source = width // tile
    steps = sources * per_source
    number = jnp.arange(steps, dtype=jnp.int32)
    kmap = (my_head - number // per_source + sources) % sources * per_source + number % per_source

    def row_map(source):
        return lambda k, m: (0, 0, jnp.clip(k - source * per_source, 0, per_source - 1))

    weight = pl.BlockSpec((1, units, tile), lambda k, m: (0, 0, m[k]))
    return pl.pallas_call(
        functools.partial(expert_in_kernel, sources, per_source),
        grid_spec=pltpu.PrefetchScalarGridSpec(
            num_scalar_prefetch=1,
            grid=(steps,),
            in_specs=[pl.BlockSpec((2, count, tile), row_map(s)) for s in range(sources)]
            + [weight] * 4,
            out_specs=pl.BlockSpec((2, count, units), lambda k, m: (0, 0, 0)),
            scratch_shapes=[pltpu.VMEM((2, count, units), F32)] * 2,
        ),
        out_shape=jax.ShapeDtypeStruct((2, count, units), BF16),
        cost_estimate=pl.CostEstimate(
            flops=8 * count * D * units,
            bytes_accessed=8 * D * units,
            transcendentals=2 * count * units,
        ),
        compiler_params=pltpu.CompilerParams(vmem_limit_bytes=24 << 20),
        name="expert_in",
    )(kmap, *rows, *weights)


def expert_out_kernel(sources, slots, *refs):
    acts = refs[:sources]
    weights = refs[sources : 3 * sources]
    outs = refs[3 * sources :]
    for e in range(2):
        total = dot(acts[0][e], weights[e * sources][...])
        for s in range(1, sources):
            total = total + dot(acts[s][e], weights[e * sources + s][...])
        total = total.astype(BF16)
        for i, out_ref in enumerate(outs):
            out_ref[e] = total[i * slots : (i + 1) * slots]


def expert_out(acts, weights, slots):
    sources = len(acts)
    _, count, units = acts[0].shape
    width = weights[0][0].shape[1]
    blocks = count // slots
    tile = min(width, 512)
    return pl.pallas_call(
        functools.partial(expert_out_kernel, sources, slots),
        grid=(width // tile,),
        in_specs=[pl.BlockSpec((2, count, units), lambda j: (0, 0, 0))] * sources
        + [pl.BlockSpec((units, tile), lambda j: (0, j))] * (2 * sources),
        out_specs=[pl.BlockSpec((2, slots, tile), lambda j: (0, 0, j))] * blocks,
        out_shape=[jax.ShapeDtypeStruct((2, slots, width), BF16)] * blocks,
        cost_estimate=pl.CostEstimate(
            flops=4 * sources * count * units * width,
            bytes_accessed=4 * sources * units * width,
            transcendentals=0,
        ),
        compiler_params=pltpu.CompilerParams(vmem_limit_bytes=16 << 20),
        name="expert_out",
    )(*acts, *weights[0], *weights[1])


def combine_kernel(first, count, slots, base_ref, gate_ref, code_ref, *refs):
    returned, out_ref = refs[:count], refs[count]
    total = base_ref[...].astype(F32)
    events = total.shape[0]
    column = lax.broadcasted_iota(jnp.int32, (events, 2 * slots), 1)
    picked = [None] * TOP
    for i, block in enumerate(returned):
        back = block[...].reshape(2 * slots, block.shape[2])
        for k in range(TOP):
            hit = column + (first + i) * 2 * slots == code_ref[:, k : k + 1]
            part = dot(jnp.where(hit, 1.0, 0.0).astype(BF16), back)
            picked[k] = part if i == 0 else picked[k] + part
    for k in range(TOP):
        total = total + picked[k] * gate_ref[:, k : k + 1]
    out_ref[...] = total.astype(out_ref.dtype)


def combine(base, gates, codes, returned, first, dtype):
    events, width = base.shape
    count, slots = len(returned), returned[0].shape[1]
    return pl.pallas_call(
        functools.partial(combine_kernel, first, count, slots),
        out_shape=jax.ShapeDtypeStruct((events, width), dtype),
        cost_estimate=pl.CostEstimate(
            flops=8 * events * count * slots * width,
            bytes_accessed=4 * count * slots * width,
            transcendentals=0,
        ),
        compiler_params=pltpu.CompilerParams(vmem_limit_bytes=16 << 20),
        name="combine",
    )(base, gates, codes, *returned)


def local(
    order,
    residual_in,
    queries,
    key_vectors,
    values,
    bar_index,
    pair_offset,
    out_proj,
    norm_gain,
    router,
    expert_route,
    w_gate,
    w_up,
    w_down,
):
    tracks = lax.axis_size("track")
    head_parts = lax.axis_size("head")
    my_track = lax.axis_index("track")
    my_head = lax.axis_index("head")
    events, width = queries.shape[1], queries.shape[2]
    chips = len(order)
    shifts = range(1, head_parts)

    barrier = lax.optimization_barrier

    forward = [
        (2 * order[i] + c, 2 * order[(i + 1) % chips] + c) for i in range(chips) for c in range(2)
    ]
    backward = [(b, a) for a, b in forward]
    hops = [0]
    for s in range(1, chips // 2):
        hops += [-s, s]
    hops.append(chips // 2)

    place = [0] * chips
    for i, chip in enumerate(order):
        place[chip] = i
    my_place = jnp.array(place, jnp.int32)[my_track // 2]
    block_chip = jnp.array(order, jnp.int32)[(my_place + jnp.array(hops, jnp.int32)) % chips]
    core = my_track % 2
    block_track = jnp.stack([block_chip * 2 + core, block_chip * 2 + 1 - core], 1).reshape(-1)
    key_bars = bar_index[block_track]
    query_track = jnp.stack([my_track, my_track ^ 1])
    query_bars = bar_index[query_track]
    partner = (query_track[:, None, None] + 1 + pair_offset[query_track]) % tracks
    listed = jnp.any(partner[:, :, :, None] == block_track, axis=2)
    listed = listed | (query_track[:, None, None] == block_track)
    listed = jnp.repeat(listed, QB, axis=1)
    query_bars = jnp.where(listed, query_bars[:, :, None], -1000)

    def columns_of(weight, owner):
        return lax.dynamic_slice_in_dim(weight, owner * width, width, 1)

    own_half, other_half = halves(core, key_vectors, values)
    streams = [[own_half], [swap_cores(other_half, tracks)]]
    own_queries, other_queries = halves(core, queries)
    both_queries = jnp.concatenate([own_queries, swap_cores(other_queries, tracks)], axis=0)
    fetched = []
    for s in shifts:
        owner = (my_head + s) % head_parts
        for part in (columns_of(out_proj, owner), columns_of(w_down[0], owner)):
            if fetched:
                part, fetched[-1] = barrier((part, fetched[-1]))
            fetched.append(shifted(part, "head", head_parts, s))
    in_weights = [jnp.swapaxes(w_gate, 1, 2), jnp.swapaxes(w_up, 1, 2)]
    in_weights += [swap_cores(w, tracks) for w in in_weights]

    steps = chips // 2
    ahead, back = [g[0] for g in streams], [g[0] for g in streams]
    for _ in range(1, steps):
        for i in range(2):
            ahead[i] = lax.ppermute(ahead[i], "track", forward)
            back[i] = lax.ppermute(back[i], "track", backward)
            streams[i] += [ahead[i], back[i]]
    streams[0].append(lax.ppermute(ahead[0], "track", forward))
    streams[1].append(lax.ppermute(back[1], "track", backward))
    kvs = [block for pair in zip(*streams, strict=True) for block in pair]

    local_heads = width // HEAD_DIM // 2
    cuts = [0, local_heads - local_heads // 2, local_heads]
    attended, weight_of, places = [], [], []
    for first, end in zip(cuts[:-1], cuts[1:], strict=True):
        mine, theirs = attention(both_queries, query_bars, key_bars, kvs, first, end - first)
        pieces = [(0, 0, mine), (0, 1, swap_cores(theirs, tracks))]
        for s in shifts:
            pieces.append((s, 0, shifted(mine, "head", head_parts, s)))
            pairs = [
                (t * head_parts + h, (t ^ 1) * head_parts + (h + s) % head_parts)
                for t in range(tracks)
                for h in range(head_parts)
            ]
            pieces.append((s, 1, lax.ppermute(theirs, ("track", "head"), pairs)))
        for s, other, piece in pieces:
            attended.append(piece)
            weight_of.append(s)
            half = 1 - core if other else core
            places.append(half * (local_heads // (end - first)) + first // (end - first))
    attended[0], fetched = barrier((attended[0], fetched))
    out_weights = [out_proj] + fetched[::2]
    down_weights = [columns_of(w_down[0], my_head)]
    for s in shifts:
        down_weights.append(fetched[2 * s - 1])
    down_weights = [down_weights, [swap_cores(w, tracks) for w in down_weights]]

    experts = tracks
    wide_router = jnp.pad(router, ((0, 0), (0, LANES - experts)))
    gain = norm_gain.reshape(1, width)
    hidden, stat = project(
        attended,
        [out_weights[s] for s in weight_of],
        jnp.stack(places + [my_head * (width // 256)]),
        residual_in[0],
        gain,
        wide_router,
        experts,
    )
    stats = [stat] + [shifted(stat, "head", head_parts, s) for s in shifts]

    slots = 2 * events * TOP // experts
    route = expert_route[0]
    flat = route.reshape(-1)
    hits = (flat[:, None] == jnp.arange(experts, dtype=jnp.int32)).astype(jnp.int32)
    rank = jnp.sum((jnp.cumsum(hits, axis=0) - hits) * hits, axis=1).reshape(events, TOP)
    tags = jnp.stack([route, rank], axis=2).reshape(events, 2 * TOP).T.astype(BF16)
    tags = jnp.pad(tags, ((0, TAG_ROWS - 2 * TOP), (0, 0)))
    hop_number = [0] * chips
    for i, hop in enumerate(hops):
        hop_number[hop % chips] = i
    hop_of_chip = jnp.array(hop_number, jnp.int32)[(my_place - jnp.array(place, jnp.int32)) % chips]
    chip_match = (route // 2)[:, :, None] == jnp.arange(chips, dtype=jnp.int32)
    hop_of_route = jnp.sum(jnp.where(chip_match, hop_of_chip, 0), axis=2)
    other_core = (route % 2 != my_track % 2).astype(jnp.int32)
    codes = (hop_of_route * 2 + other_core) * slots + rank
    my_experts = jnp.stack([my_track, my_track ^ 1])

    in_weights = [pltpu.with_memory_space_constraint(w, pltpu.VMEM) for w in in_weights]
    down_weights = [
        [pltpu.with_memory_space_constraint(w, pltpu.VMEM) for w in ws] for ws in down_weights
    ]
    block, gates = pack(hidden, stats, gain, route, tags, experts)
    ends = [chips * share // 8 for share in EXPERT_GROUPS]
    blocks, forth, back = [block], block, block
    picked, ready = [], []
    for step in range(1, chips // 2 + 1):
        for group, when in enumerate(ready):
            if when == step - 2:
                forth, back, picked[group] = barrier((forth, back, picked[group]))
        forth = lax.ppermute(forth, "track", forward)
        blocks.append(forth)
        if step < chips // 2:
            back = lax.ppermute(back, "track", backward)
            blocks.append(back)
        while len(picked) < len(ends) and len(blocks) >= ends[len(picked)]:
            first = ends[len(picked) - 1] if picked else 0
            picked.append(select(my_experts, blocks[first : ends[len(picked)]], slots))
            ready.append(step)

    def across(x):
        return [x] + [shifted(x, "head", head_parts, s) for s in shifts]

    acts, returned, waiting, first = [], [], None, 0
    starts = [0] + ends[:-1]
    for group in range(len(ends) + 1):
        if group < len(ends):
            rows = across(picked[group])
            if waiting is not None:
                rows, waiting = barrier((rows, waiting))
            acts.append(across(expert_in(rows, in_weights, my_head)))
        if group > 0:
            outs = expert_out(acts[group - 1], down_weights, slots)
            for i, out in enumerate(outs):
                hop_length = hops[starts[group - 1] + i]
                pairs = [
                    (2 * order[p] + c, 2 * order[(p + hop_length) % chips] + c)
                    for p in range(chips)
                    for c in range(2)
                ]
                returned.append(lax.ppermute(out, "track", pairs) if hop_length else out)
            waiting = outs[0]
    result = combine(hidden, gates, codes, returned[: starts[-1]], 0, F32)
    result = combine(result, gates, codes, returned[starts[-1] :], starts[-1], BF16)
    return result[None]


def solution(mesh):
    chips, columns = mesh.shape["track"] // 2, mesh.shape["head"]
    order = chip_ring(chips // columns, columns)
    in_specs = (
        P("track", None, "head"),
        P("track", None, "head"),
        P("track", None, "head"),
        P("track", None, "head"),
        P(),
        P(),
        P("head", None),
        P("head"),
        P("head", None),
        P("track", None, None),
        P("track", None, "head"),
        P("track", None, "head"),
        P("track", "head", None),
    )
    out_specs = P("track", None, "head")
    return jax.shard_map(
        functools.partial(local, order),
        mesh=mesh,
        in_specs=in_specs,
        out_specs=out_specs,
        check_vma=False,
    )
```
